128 devices in a mesh: seq: 16 (over x, y), segment: 8 (over z, core).
Axes of the slice: x: 4, y: 4, z: 4, core: 2. Of those that a mesh axis runs over, the one named last changes fastest.
Arguments:
- base_state: bfloat16 [2048, 1024], P('seq'), may hold values from -6 to 6
- forcing: float32 [2048, 64], P('seq'), may hold values from -6 to 6
- theta_base: float32 [64], replicated, may hold values from -1 to 1
- perturb: float32 [32, 64], replicated, may hold values from -6 to 6
- order: int32 [32], replicated, may hold values from 0 to 31, each once
- w_force: bfloat16 [64, 1024], replicated, may hold values from -0.75 to 0.75
- attn_gain: float32 [8, 1024], P('segment'), may hold values from 0.25 to 1.75
- w_query: bfloat16 [8, 1024, 1024], P('segment'), may hold values from -16 to 16
- w_key: bfloat16 [8, 1024, 1024], P('segment'), may hold values from -1 to 1, as said below
- w_value: bfloat16 [8, 1024, 1024], P('segment'), may hold values from -0.1875 to 0.1875
- w_out: bfloat16 [8, 1024, 1024], P('segment'), may hold values from -0.1875 to 0.1875
- block_mask: int32 [16, 4], P('seq'), may hold values 0 or 1
- out_gain: float32 [1024], replicated, may hold values from 0.25 to 1.75
- w_read: bfloat16 [1024, 128], replicated, may hold values from -0.1875 to 0.1875
- observed: float32 [2048, 128], P('seq'), may hold values from -8 to 8
Outputs:
- predictions: float32 [8, 2048, 128], P('segment', 'seq')
- fitness: float32 [8], P('segment')
The draws below stay inside these ranges and needn't reach their ends.
Inputs may be any that keep to these rules, and one draw needn't show every extreme that they name: `order`: each pool index appears once. `w_key`: a projection matrix of order one over square root of 1024.
All inputs are finite; a program needn't handle non-finite values. No bound on the sum of `block_mask` on one device may be relied on, other than what follows from the above.
Results may differ from the reference program's by a relative error of at most 0.02.
Values may be sent and summed in bfloat16 or wider, within the bound.
A program may use at most 64 MiB of HBM per device.

```python
import math
import jax
import jax.numpy as jnp
from jax import lax

D = 1024
HEADS = 16
PARAMS = 64
CHANNELS = 128
LEVELS = 4
NBLK = 16
SEQ_LEN = 2048
SECTIONS = 8
MEMBERS = 8
POOL = 32


def shared_keys(key):
    return jax.random.normal(jax.random.fold_in(key, 7), (SECTIONS, D, D), jnp.float32) / math.sqrt(D)


def draw_w_key(key, part):
    return shared_keys(key).astype(jnp.bfloat16)


def draw_w_query(key, part):
    fresh = jax.random.normal(jax.random.fold_in(key, 8), (SECTIONS, D, D), jnp.float32) / math.sqrt(D)
    return fresh.astype(jnp.bfloat16)


def draw_observed(key, part):
    level = jax.random.uniform(jax.random.fold_in(key, 11), (), jnp.float32, -1.5, 1.5)
    channel_level = jax.random.uniform(jax.random.fold_in(key, 12), (1, CHANNELS), jnp.float32, -0.75, 0.75)
    rough = jnp.clip(jax.random.normal(jax.random.fold_in(key, 13), (SEQ_LEN, CHANNELS), jnp.float32), -5.5, 5.5)
    return rough + level + channel_level


def plant(array, own_key, smallest, high):
    longest = array.shape.index(max(array.shape))
    spots = []
    for shift in (0, 1):
        where = [jax.random.randint(jax.random.fold_in(own_key, axis), (), 0, length) for axis, length in enumerate(array.shape)]
        where[longest] = (where[longest] + shift) % array.shape[longest]
        spots.append(tuple(where))
    return array.at[spots[0]].set(smallest).at[spots[1]].set(high)


def block_levels(key, dims, split, smallest, top_value):
    def one(axis_at, blocks):
        draws = jax.random.uniform(jax.random.fold_in(jax.random.fold_in(key, 6), axis_at), (blocks,), jnp.float32, smallest / len(split), top_value / len(split))
        return jnp.repeat(jnp.exp(draws), dims[axis_at] // blocks).reshape((-1,) + (1,) * (len(dims) - axis_at - 1))

    level = one(*split[0])
    for cut in split[1:]:
        level = level * one(*cut)
    return level


def noise(own_key, dims, spread, reach, pieces=(), held_as=jnp.bfloat16):
    level = block_levels(own_key, dims, pieces, -0.22, 0.18) if pieces else 1.0
    drawn = jax.random.normal(own_key, dims, jnp.float32) * spread * level
    return jnp.minimum(jnp.maximum(drawn, -reach), reach).astype(held_as)


def setup_inputs(seed: int = 0) -> dict:
    key_of = jax.random.split(jax.random.key(seed), 16)
    return {
        "base_state": noise(key_of[0], (SEQ_LEN, D), 1.0, 6.0, ((0, 16),)),
        "forcing": noise(key_of[1], (SEQ_LEN, PARAMS), 1.0, 6.0, ((0, 16),), jnp.float32),
        "theta_base": jnp.clip(jax.random.uniform(key_of[2], (PARAMS,), jnp.float32, -1.0, 1.0), -1.0, 1.0),
        "perturb": noise(key_of[3], (POOL, PARAMS), 1.0, 6.0, (), jnp.float32),
        "order": jax.random.permutation(key_of[4], POOL).astype(jnp.int32),
        "w_force": noise(key_of[5], (PARAMS, D), PARAMS ** -0.5, 0.75),
        "attn_gain": jnp.clip(1.0 + 0.15 * jax.random.normal(key_of[6], (SECTIONS, D), jnp.float32), 0.25, 1.75),
        "w_query": draw_w_query(jax.random.fold_in(key_of[15], 71), 0),
        "w_key": draw_w_key(jax.random.fold_in(key_of[15], 71), 0),
        "w_value": noise(key_of[9], (SECTIONS, D, D), D ** -0.5, 0.1875, ((0, 8),)),
        "w_out": noise(key_of[10], (SECTIONS, D, D), D ** -0.5, 0.1875, ((0, 8),)),
        "block_mask": plant((jax.random.randint(key_of[11], (NBLK, LEVELS), 0, 4) < 3).astype(jnp.int32), jax.random.fold_in(key_of[11], 1), 0, 1),
        "out_gain": jnp.clip(1.0 + 0.15 * jax.random.normal(key_of[12], (D,), jnp.float32), 0.25, 1.75),
        "w_read": noise(key_of[13], (D, CHANNELS), D ** -0.5, 0.1875),
        "observed": draw_observed(jax.random.fold_in(key_of[15], 71), 0),
    }


def norm_rows(state, gain):
    values = state.astype(jnp.float32)
    meansq = lax.optimization_barrier(jnp.mean(values * values, axis=-1, keepdims=True)) + 1e-05
    return (values * lax.rsqrt(meansq) * gain).astype(jnp.bfloat16)

def attend(queries, keys_all, values_all, visible):
    rows = queries.shape[0]
    count = keys_all.shape[0]
    qhead = queries.astype(jnp.float32).reshape(rows, HEADS, -1)
    khead = keys_all.astype(jnp.float32).reshape(count, HEADS, -1)
    vhead = values_all.astype(jnp.float32).reshape(count, HEADS, -1)
    scores = jnp.einsum('qhe,khe->hqk', qhead, khead) * 0.125
    scores = jnp.where(visible[None], scores, -1e+30)
    peak = lax.optimization_barrier(jnp.max(scores, axis=-1, keepdims=True))
    expon = jnp.exp(scores - peak)
    weights = (expon / lax.optimization_barrier(jnp.sum(expon, axis=-1, keepdims=True))).astype(jnp.bfloat16)
    context = jnp.einsum('hqk,khe->qhe', weights.astype(jnp.float32), vhead)
    return context.reshape(rows, -1).astype(jnp.bfloat16)

def section(state, gain, wq, wk, wv, wo, mask):
    length, width = state.shape
    blocks = mask.shape[0]
    block_rows = length // blocks
    normed = norm_rows(state, gain)
    queries = jnp.dot(normed, wq, preferred_element_type=jnp.float32).astype(jnp.bfloat16)
    keys_loc = jnp.dot(normed, wk, preferred_element_type=jnp.float32).astype(jnp.bfloat16)
    values_loc = jnp.dot(normed, wv, preferred_element_type=jnp.float32).astype(jnp.bfloat16)
    qblock = queries.reshape(blocks, block_rows, width)
    kblock = keys_loc.reshape(blocks, block_rows, width)
    vblock = values_loc.reshape(blocks, block_rows, width)
    causal = jnp.arange(block_rows)[:, None] >= jnp.arange(block_rows)[None, :]
    key_parts = [kblock]
    value_parts = [vblock]
    visible_parts = [jnp.broadcast_to(causal, (blocks, block_rows, block_rows))]
    block_ids = jnp.arange(blocks)
    for level in range(LEVELS):
        offset = 2 ** level
        if offset < blocks:
            padding = jnp.zeros((offset, block_rows, width), jnp.bfloat16)
            key_parts.append(jnp.concatenate([padding, kblock[:-offset]], axis=0))
            value_parts.append(jnp.concatenate([padding, vblock[:-offset]], axis=0))
            usable = (mask[:, level] == 1) & (block_ids >= offset)
            visible_parts.append(jnp.broadcast_to(usable[:, None, None], (blocks, block_rows, block_rows)))
    keys_all = jnp.concatenate(key_parts, axis=1)
    values_all = jnp.concatenate(value_parts, axis=1)
    visible = jnp.concatenate(visible_parts, axis=2)
    context = lax.map(lambda item: attend(item[0], item[1], item[2], item[3]), (qblock, keys_all, values_all, visible))
    mixed = state.astype(jnp.float32) + jnp.dot(context.reshape(length, width), wo, preferred_element_type=jnp.float32)
    return mixed.astype(jnp.bfloat16)

def reference(base_state, forcing, theta_base, perturb, order, w_force, attn_gain, w_query, w_key, w_value, w_out, block_mask, out_gain, w_read, observed):
    theta = theta_base[None, :] + 0.5 * perturb[order[:MEMBERS]]
    length = base_state.shape[0]
    channels = observed.shape[1]
    hour_weight = 1.0 + 2.0 * jnp.arange(length).astype(jnp.float32) / (length - 1)
    outputs = []
    scores_all = []
    for slot in range(MEMBERS):
        drive = forcing * theta[slot][None, :]
        state = (base_state.astype(jnp.float32) + jnp.dot(drive, w_force.astype(jnp.float32), precision=lax.Precision.HIGHEST)).astype(jnp.bfloat16)
        for index in range(SECTIONS):
            state = section(state, attn_gain[index], w_query[index], w_key[index], w_value[index], w_out[index], block_mask)
        predicted = jnp.dot(norm_rows(state, out_gain), w_read, preferred_element_type=jnp.float32)
        errors = predicted - observed
        outputs.append(predicted)
        scores_all.append(-jnp.sum(hour_weight[:, None] * errors * errors) / (length * channels))
    return (jnp.stack(outputs), jnp.stack(scores_all))
```

```python
import jax
import jax.numpy as jnp
from jax import lax
from jax.experimental import pallas as pl
from jax.experimental.pallas import tpu as pltpu
from jax.sharding import PartitionSpec as P

TICKS = 8
PAIRS = 8
CHUNKS = 4
AHEAD = 2
NEG = -1e30


def rms(values, gain):
    meansq = jnp.mean(values * values, axis=-1, keepdims=True) + 1e-05
    return (values * lax.rsqrt(meansq) * gain).astype(jnp.bfloat16)


def rows_of(ref):
    return jnp.concatenate([ref[c] for c in range(CHUNKS)], axis=1)


def kernel(
    base_ref,
    forcing_ref,
    theta_ref,
    perturb_ref,
    order_ref,
    w_force_ref,
    gain_ref,
    wq_hbm,
    wk_hbm,
    wv_hbm,
    wo_hbm,
    mask_ref,
    out_gain_ref,
    w_read_ref,
    observed_ref,
    pred_out,
    fit_out,
    wq,
    wk,
    wv,
    wo,
    x_own,
    x_cross,
    x_out,
    starts,
    normed,
    q_buf,
    k_own,
    v_own,
    k_cross,
    v_cross,
    ctx,
    causal,
    bias,
    obs,
    pred_send,
    pred_recv,
    acc,
    fit_send,
    fit_recv,
    w_sem,
    own_sem,
    cross_sem,
    send_own_sem,
    send_cross_sem,
    start_sem,
    bias_sem,
    bias_send_sem,
    obs_sem,
    obs_send_sem,
    pred_sem,
    pred_send_sem,
    fit_sem,
    fit_send_sem,
):
    seq = lax.axis_index("seq")
    seg = lax.axis_index("segment")
    lane = seq % 2
    member = seq // 2
    home = seq // 2
    other = seq + 1 - 2 * lane
    last = 7

    def remote(src, dst, send, recv, to_seq, to_seg):
        return pltpu.make_async_remote_copy(
            src_ref=src,
            dst_ref=dst,
            send_sem=send,
            recv_sem=recv,
            device_id={"seq": to_seq, "segment": to_seg},
            device_id_type=pl.DeviceIdType.MESH,
        )

    loads = [
        pltpu.make_async_copy(hbm.at[0], vmem, w_sem.at[i])
        for i, (hbm, vmem) in enumerate(((wq_hbm, wq), (wk_hbm, wk), (wv_hbm, wv), (wo_hbm, wo)))
    ]
    for load in loads:
        load.start()

    def send_start(m, _):
        target = 2 * m + lane

        @pl.when(target != seq)
        def _():
            remote(
                starts.at[m], x_own.at[home], start_sem.at[m], own_sem.at[home], target, 0
            ).start()

        return 0

    def make_start(m, _):
        theta = theta_ref[...] + 0.5 * perturb_ref[pl.ds(order_ref[m], 1), :]
        drive = forcing_ref[...] * theta
        high = drive.astype(jnp.bfloat16)
        rest = drive - high.astype(jnp.float32)
        middle = rest.astype(jnp.bfloat16)
        low = (rest - middle.astype(jnp.float32)).astype(jnp.bfloat16)
        for c in range(CHUNKS):
            columns = slice(256 * c, 256 * (c + 1))
            w = w_force_ref[:, columns]
            lifted = jnp.dot(low, w, preferred_element_type=jnp.float32)
            lifted += jnp.dot(middle, w, preferred_element_type=jnp.float32)
            lifted += jnp.dot(high, w, preferred_element_type=jnp.float32)
            starts[m, c] = (base_ref[:, columns].astype(jnp.float32) + lifted).astype(jnp.bfloat16)

        @pl.when(home < AHEAD)
        def _():
            send_start(m, 0)

        return 0

    @pl.when(seg == 0)
    def _():
        lax.fori_loop(0, 8, make_start, 0)
        x_own[home] = starts[member]

    for level in range(4):
        usable = (mask_ref[0, level] == 1) & (seq >= 2**level)
        row = jnp.full((8, 128), jnp.where(usable, 0.0, NEG), jnp.float32)
        bias[home, :, 128 * level : 128 * (level + 1)] = row

    def send_bias(j, _):
        target = 2 * j + lane

        @pl.when(target != seq)
        def _():
            remote(
                bias.at[home], bias.at[home], bias_send_sem.at[j], bias_sem.at[home], target, seg
            ).start()

        return 0

    lax.fori_loop(0, 8, send_bias, 0)

    def send_obs(j, _):
        target = 2 * j + lane

        @pl.when(target != seq)
        def _():
            remote(
                obs.at[home], obs.at[home], obs_send_sem.at[j], obs_sem.at[home], target, last
            ).start()

        return 0

    @pl.when(seg == last)
    def _():
        obs[home] = observed_ref[...]
        lax.fori_loop(0, 8, send_obs, 0)

    row = lax.broadcasted_iota(jnp.int32, (256, 128), 0) % 128
    column = lax.broadcasted_iota(jnp.int32, (256, 128), 1)
    causal[...] = jnp.where(column <= row, 0.0, NEG)
    acc[...] = jnp.zeros_like(acc)

    @pl.when(lane == 0)
    def _():
        x_cross[0] = jnp.zeros_like(x_cross[0])

    for load in loads:
        load.wait()

    left = lax.broadcasted_iota(jnp.int32, (128, 128), 1) < 64
    ones = jnp.ones((640, 128), jnp.bfloat16)

    def tick(t, _):
        @pl.when((seg == 0) & (home >= AHEAD) & (t == home - AHEAD))
        def _():
            lax.fori_loop(0, 8, send_start, 0)

        @pl.when((seg > 0) | (t != home))
        def _():
            pltpu.make_async_copy(x_own.at[t], x_own.at[t], own_sem.at[t]).wait()

        @pl.when((seg == 0) & (t + lane < TICKS))
        def _():
            remote(
                x_own.at[t],
                x_cross.at[t + lane],
                send_cross_sem.at[t],
                cross_sem.at[t + lane],
                other,
                0,
            ).start()

        x = rows_of(x_own.at[t]).astype(jnp.float32)
        gain = gain_ref[...]
        normed[0:128] = rms(x, gain)

        @pl.when((lane == 1) | (t > 0))
        def _():
            pltpu.make_async_copy(x_cross.at[t], x_cross.at[t], cross_sem.at[t]).wait()

        normed[128:256] = rms(rows_of(x_cross.at[t]).astype(jnp.float32), gain)

        for c in range(CHUNKS):
            columns = slice(256 * c, 256 * (c + 1))
            q = jnp.dot(normed[0:128], wq[:, columns], preferred_element_type=jnp.float32) * 0.125
            k = jnp.dot(normed[...], wk[:, columns], preferred_element_type=jnp.float32)
            v = jnp.dot(normed[...], wv[:, columns], preferred_element_type=jnp.float32)
            for i in range(2):
                p = 2 * c + i
                part = slice(128 * i, 128 * (i + 1))
                q_buf[p, 0:128] = jnp.where(left, q[:, part], 0.0).astype(jnp.bfloat16)
                q_buf[p, 128:256] = jnp.where(left, 0.0, q[:, part]).astype(jnp.bfloat16)
                k_own[t, p] = k[0:128, part].astype(jnp.bfloat16)
                k_cross[p] = k[128:256, part].astype(jnp.bfloat16)
                v_own[t, p] = v[0:128, part].astype(jnp.bfloat16)
                v_cross[p] = v[128:256, part].astype(jnp.bfloat16)

        @pl.when(t != home)
        def _():
            pltpu.make_async_copy(bias.at[t], bias.at[t], bias_sem.at[t]).wait()

        behind = [jnp.maximum(t - offset, 0) for offset in (1, 2, 4)]

        def attend(p):
            keys = jnp.concatenate(
                [k_own[t, p], k_cross[p]] + [k_own[index, p] for index in behind], axis=0
            )
            values = jnp.concatenate(
                [v_own[t, p], v_cross[p]] + [v_own[index, p] for index in behind], axis=0
            )
            scores = lax.dot_general(
                q_buf[p], keys, (((1,), (1,)), ((), ())), preferred_element_type=jnp.float32
            )
            scores = jnp.concatenate(
                [scores[:, 0:128] + causal[...], scores[:, 128:640] + bias[t, 0:1, :]], axis=1
            )
            peak = jnp.max(scores, axis=-1, keepdims=True)
            expon = jnp.exp(scores - peak).astype(jnp.bfloat16)
            both = jnp.dot(
                expon, jnp.concatenate([values, ones], axis=1), preferred_element_type=jnp.float32
            )
            mixed = both[:, 0:128] / both[:, 128:256]
            ctx[p] = jnp.where(left, mixed[0:128], mixed[128:256]).astype(jnp.bfloat16)

        def attend_two(i, _):
            attend(2 * i)
            attend(2 * i + 1)
            return 0

        lax.fori_loop(0, PAIRS // 2, attend_two, 0)

        context = jnp.concatenate([ctx[p] for p in range(PAIRS)], axis=1)
        for c in range(CHUNKS):
            columns = slice(256 * c, 256 * (c + 1))
            mixed = jnp.dot(context, wo[:, columns], preferred_element_type=jnp.float32)
            x_out[t, c] = (x_own[t, c].astype(jnp.float32) + mixed).astype(jnp.bfloat16)

            @pl.when(seg < last)
            def _():
                remote(
                    x_out.at[t, c], x_own.at[t, c], send_own_sem.at[t], own_sem.at[t], seq, seg + 1
                ).start()

            @pl.when((seg < last) & (t + lane < TICKS))
            def _():
                remote(
                    x_out.at[t, c],
                    x_cross.at[t + lane, c],
                    send_cross_sem.at[t + TICKS],
                    cross_sem.at[t + lane],
                    other,
                    seg + 1,
                ).start()

        @pl.when(seg == last)
        def _():
            final = rms(rows_of(x_out.at[t]).astype(jnp.float32), out_gain_ref[...])
            predicted = jnp.dot(final, w_read_ref[...], preferred_element_type=jnp.float32)
            block = 2 * t + lane
            pred_send[t] = predicted

            @pl.when((block != seq) | (member != last))
            def _():
                remote(
                    pred_send.at[t], pred_recv, pred_send_sem.at[t], pred_sem, block, member
                ).start()

            @pl.when((block == seq) & (member == last))
            def _():
                pred_recv[...] = predicted

            @pl.when(t != home)
            def _():
                pltpu.make_async_copy(obs.at[t], obs.at[t], obs_sem.at[t]).wait()

            errors = predicted - obs[t]
            hours = lax.broadcasted_iota(jnp.int32, (128, 128), 0) + block * 128
            weight = 1.0 + hours.astype(jnp.float32) * (2.0 / 2047.0)
            squares = weight * errors * errors
            acc[...] += jnp.sum(squares.reshape(16, 8, 128), axis=0)

        return 0

    lax.fori_loop(0, TICKS, tick, 0)

    def send_fit(j, _):
        @pl.when((j != seq) | (member != last))
        def _():
            remote(
                fit_send, fit_recv.at[lane], fit_send_sem.at[j], fit_sem.at[lane], j, member
            ).start()

        return 0

    def sent_fit(j, _):
        @pl.when((j != seq) | (member != last))
        def _():
            remote(
                fit_send, fit_recv.at[lane], fit_send_sem.at[j], fit_sem.at[lane], j, member
            ).wait_send()

        return 0

    @pl.when(seg == last)
    def _():
        fit_send[...] = acc[...]
        lax.fori_loop(0, 16, send_fit, 0)

        @pl.when(member == last)
        def _():
            fit_recv[lane] = acc[...]

    def sent_tick(t, _):
        @pl.when(seg < last)
        def _():
            pltpu.make_async_copy(x_out.at[t], x_out.at[t], send_own_sem.at[t]).wait()

            @pl.when(t + lane < TICKS)
            def _():
                pltpu.make_async_copy(x_out.at[t], x_out.at[t], send_cross_sem.at[t + TICKS]).wait()

        @pl.when((seg == 0) & (t + lane < TICKS))
        def _():
            pltpu.make_async_copy(x_own.at[t], x_own.at[t], send_cross_sem.at[t]).wait()

        @pl.when((seg == 0) & (2 * t + lane != seq))
        def _():
            pltpu.make_async_copy(starts.at[t], starts.at[t], start_sem.at[t]).wait()

        @pl.when(2 * t + lane != seq)
        def _():
            pltpu.make_async_copy(bias.at[home], bias.at[home], bias_send_sem.at[t]).wait()

        @pl.when(seg == last)
        def _():
            @pl.when(2 * t + lane != seq)
            def _():
                pltpu.make_async_copy(obs.at[home], obs.at[home], obs_send_sem.at[t]).wait()

            @pl.when((2 * t + lane != seq) | (member != last))
            def _():
                pltpu.make_async_copy(pred_send.at[t], pred_send.at[t], pred_send_sem.at[t]).wait()

        return 0

    lax.fori_loop(0, TICKS, sent_tick, 0)

    @pl.when(seg == last)
    def _():
        lax.fori_loop(0, 16, sent_fit, 0)

    @pl.when((seg != last) | (member != last))
    def _():
        pltpu.make_async_copy(pred_recv, pred_recv, pred_sem).wait()

    for source in range(2):

        @pl.when((seg != last) | (seq != 14 + source))
        def _():
            pltpu.make_async_copy(fit_recv.at[source], fit_recv.at[source], fit_sem.at[source]).wait()

    pred_out[...] = pred_recv[...]
    total = jnp.sum(fit_recv[0] + fit_recv[1])
    fit_out[0] = -total / (2048.0 * 128.0)


def per_device(
    base_state,
    forcing,
    theta_base,
    perturb,
    order,
    w_force,
    attn_gain,
    w_query,
    w_key,
    w_value,
    w_out,
    block_mask,
    out_gain,
    w_read,
    observed,
):
    vmem = pl.BlockSpec(memory_space=pltpu.VMEM)
    smem = pl.BlockSpec(memory_space=pltpu.SMEM)
    hbm = pl.BlockSpec(memory_space=pl.ANY)
    bf16, f32 = jnp.bfloat16, jnp.float32
    dma = pltpu.SemaphoreType.DMA
    predictions, fitness = pl.pallas_call(
        kernel,
        out_shape=(
            jax.ShapeDtypeStruct((128, 128), f32),
            jax.ShapeDtypeStruct((1,), f32),
        ),
        in_specs=[vmem, vmem, vmem, vmem, smem, vmem, vmem, hbm, hbm, hbm, hbm, smem, vmem, vmem, vmem],
        out_specs=(vmem, smem),
        scratch_shapes=[
            pltpu.VMEM((1024, 1024), bf16),
            pltpu.VMEM((1024, 1024), bf16),
            pltpu.VMEM((1024, 1024), bf16),
            pltpu.VMEM((1024, 1024), bf16),
            pltpu.VMEM((TICKS, CHUNKS, 128, 256), bf16),
            pltpu.VMEM((TICKS, CHUNKS, 128, 256), bf16),
            pltpu.VMEM((TICKS, CHUNKS, 128, 256), bf16),
            pltpu.VMEM((8, CHUNKS, 128, 256), bf16),
            pltpu.VMEM((256, 1024), bf16),
            pltpu.VMEM((PAIRS, 256, 128), bf16),
            pltpu.VMEM((TICKS, PAIRS, 128, 128), bf16),
            pltpu.VMEM((TICKS, PAIRS, 128, 128), bf16),
            pltpu.VMEM((PAIRS, 128, 128), bf16),
            pltpu.VMEM((PAIRS, 128, 128), bf16),
            pltpu.VMEM((PAIRS, 128, 128), bf16),
            pltpu.VMEM((256, 128), f32),
            pltpu.VMEM((TICKS, 8, 512), f32),
            pltpu.VMEM((TICKS, 128, 128), f32),
            pltpu.VMEM((TICKS, 128, 128), f32),
            pltpu.VMEM((128, 128), f32),
            pltpu.VMEM((8, 128), f32),
            pltpu.VMEM((8, 128), f32),
            pltpu.VMEM((2, 8, 128), f32),
            dma((4,)),
            dma((TICKS,)),
            dma((TICKS,)),
            dma((TICKS,)),
            dma((2 * TICKS,)),
            dma((8,)),
            dma((TICKS,)),
            dma((8,)),
            dma((TICKS,)),
            dma((8,)),
            dma,
            dma((TICKS,)),
            dma((2,)),
            dma((16,)),
        ],
        compiler_params=pltpu.CompilerParams(
            has_side_effects=True, vmem_limit_bytes=48 * 1024 * 1024
        ),
    )(
        base_state,
        forcing,
        theta_base.reshape(1, -1),
        perturb,
        order,
        w_force,
        attn_gain,
        w_query,
        w_key,
        w_value,
        w_out,
        block_mask,
        out_gain.reshape(1, -1),
        w_read,
        observed,
    )
    return predictions[None], fitness


def solution(mesh):
    placed = (
        P("seq", None),
        P("seq", None),
        P(),
        P(),
        P(),
        P(),
        P("segment", None),
        P("segment", None, None),
        P("segment", None, None),
        P("segment", None, None),
        P("segment", None, None),
        P("seq", None),
        P(),
        P(),
        P("seq", None),
    )
    return jax.shard_map(
        per_device,
        mesh=mesh,
        in_specs=placed,
        out_specs=(P("segment", "seq", None), P("segment")),
        check_vma=False,
    )
```

```python
import jax
import jax.numpy as jnp
from jax import lax
from jax.experimental import pallas as pl
from jax.experimental.pallas import tpu as pltpu
from jax.sharding import PartitionSpec as P

TICKS = 8
PAIRS = 8
CHUNKS = 4
UNROLL = 4
NEG = -1e30


def rms(values, gain):
    meansq = jnp.mean(values * values, axis=-1, keepdims=True) + 1e-05
    return (values * lax.rsqrt(meansq) * gain).astype(jnp.bfloat16)


def rows_of(ref):
    return jnp.concatenate([ref[c] for c in range(CHUNKS)], axis=1)


def kernel(
    base_hbm,
    forcing_hbm,
    theta_hbm,
    perturb_hbm,
    order_hbm,
    w_force_hbm,
    gain_hbm,
    wq_hbm,
    wk_hbm,
    wv_hbm,
    wo_hbm,
    mask_hbm,
    out_gain_hbm,
    w_read_hbm,
    observed_hbm,
    pred_out,
    fit_out,
    base_ref,
    forcing_ref,
    theta_ref,
    perturb_ref,
    order_ref,
    w_force_ref,
    gain_ref,
    mask_ref,
    out_gain_ref,
    w_read_ref,
    wq,
    wk,
    wv,
    wo,
    x_own,
    x_out,
    start,
    normed,
    q_buf,
    k_own,
    v_own,
    k_cross,
    v_cross,
    ctx,
    causal,
    bias,
    obs,
    pred_send,
    pred_recv,
    acc,
    fit_send,
    fit_recv,
    load_sem,
    w_sem,
    w_send_sem,
    own_sem,
    send_own_sem,
    cross_sem,
    send_cross_sem,
    start_sem,
    bias_sem,
    bias_send_sem,
    obs_sem,
    obs_send_sem,
    pred_sem,
    pred_send_sem,
    fit_sem,
    fit_send_sem,
    token,
):
    seq = lax.axis_index("seq")
    seg = lax.axis_index("segment")
    member = seq // 2
    place = seq % 2
    plane = seg // 2
    lane = seg % 2
    sibling = seg + 1 - 2 * lane
    second = (place + plane) % 2
    stage = 2 * plane + second
    owner = lane == second
    last = 7
    next_seq = seq + (1 - second) * (1 - 2 * place)
    next_seg = seg + 2 * second
    home = seq // 2
    slot = 2 * ((plane + 8 - home) % 4) + lane
    parity = seq % 2
    is_start = seq + seg == 0
    keeps = parity == lane
    final = (stage == last) & (place == 0)

    def peer(to_seq, to_seg):
        return {"seq": to_seq, "segment": to_seg}

    def remote(src, dst, send, recv, to_seq, to_seg):
        return pltpu.make_async_remote_copy(
            src_ref=src,
            dst_ref=dst,
            send_sem=send,
            recv_sem=recv,
            device_id=peer(to_seq, to_seg),
            device_id_type=pl.DeviceIdType.MESH,
        )

    def arrived(ref, sem):
        pltpu.make_async_copy(ref, ref, sem).wait()

    def signal(sem, to_seq, to_seg):
        pl.semaphore_signal(
            sem, inc=1, device_id=peer(to_seq, to_seg), device_id_type=pl.DeviceIdType.MESH
        )

    first = [
        (base_hbm, base_ref),
        (forcing_hbm, forcing_ref),
        (theta_hbm, theta_ref),
        (perturb_hbm, perturb_ref),
        (order_hbm, order_ref),
        (w_force_hbm, w_force_ref),
        (mask_hbm, mask_ref),
        (out_gain_hbm, out_gain_ref),
        (w_read_hbm, w_read_ref),
    ]
    own_obs = pltpu.make_async_copy(observed_hbm, obs.at[home], load_sem.at[len(first)])
    loads = [
        pltpu.make_async_copy(source, target, load_sem.at[i])
        for i, (source, target) in enumerate(first)
    ]
    for load in loads:
        load.start()

    @pl.when(keeps)
    def _():
        own_obs.start()

    weights = [
        (gain_hbm, gain_ref),
        (wk_hbm.at[0], wk),
        (wv_hbm.at[0], wv),
        (wq_hbm.at[0], wq),
        (wo_hbm.at[0], wo),
    ]

    @pl.when(owner)
    def _():
        for i, (source, target) in enumerate(weights):
            pltpu.make_async_copy(source, target, w_sem.at[i]).start()

    barrier = pltpu.get_barrier_semaphore()
    signal(barrier, seq, sibling)

    @pl.when(stage > 0)
    def _():
        signal(barrier, seq + second * (1 - 2 * place), seg - 2 * (1 - second))

    def greet(t, _):
        source = 2 * t + lane

        @pl.when(source != seq)
        def _():
            signal(barrier, source, seg)

            @pl.when(final)
            def _():
                signal(barrier, source, seg)

        @pl.when((stage == 0) & ((seq + seg > 0) | (t > 0)))
        def _():
            signal(barrier, source, 2 * ((member // 2 + t) % 4) + member % 2)

        return 0

    lax.fori_loop(0, TICKS, greet, 0)

    before = home - 3 + plane // 3
    after = home + 3 - (plane % 2) * (1 - plane // 3)
    follows = (plane > 0) & (before >= 0)
    leads = (plane > 0) & (after < 8)
    before_seg = 2 * (plane % 3 + 1) + lane
    after_seg = 2 * ((plane + 1) % 3 + 1) + lane

    @pl.when(follows)
    def _():
        signal(barrier, 2 * before + parity, before_seg)

    for source in range(2):

        @pl.when((seq != 2 * seg) | (seg != 6 + source))
        def _():
            signal(barrier, 2 * seg, 6 + source)

    ends = stage // last
    apart = ((member - seg) * (member - seg) + 63) // 64
    expected = 2 - ends + (seq + seg + 126) // 127
    expected += ((plane + 2) // 3) * (1 - after // 8)
    expected += (1 - (parity + lane) % 2) * (15 + (plane // 3) * (7 + lane))
    expected += ends * (15 + apart)
    pl.semaphore_wait(barrier, expected)

    @pl.when(owner)
    def _():
        for i, (source, target) in enumerate(weights):
            remote(source, target, w_send_sem.at[i], w_sem.at[i], seq, sibling).start()

    for load in loads:
        load.wait()

    def start_copy():
        return remote(start, x_own.at[home], start_sem, own_sem.at[home], 2 * slot, parity)

    theta = theta_ref[...] + 0.5 * perturb_ref[pl.ds(order_ref[slot], 1), :]
    drive = forcing_ref[...].T * theta
    high = drive.astype(jnp.bfloat16)
    rest = drive - high.astype(jnp.float32)
    middle = rest.astype(jnp.bfloat16)
    low = (rest - middle.astype(jnp.float32)).astype(jnp.bfloat16)
    for c in range(CHUNKS):
        columns = slice(256 * c, 256 * (c + 1))
        w = w_force_ref[:, columns]
        lifted = jnp.dot(low, w, preferred_element_type=jnp.float32)
        lifted += jnp.dot(middle, w, preferred_element_type=jnp.float32)
        lifted += jnp.dot(high, w, preferred_element_type=jnp.float32)
        start[c] = (base_ref[:, columns].astype(jnp.float32) + lifted).astype(jnp.bfloat16)

    @pl.when(is_start)
    def _():
        x_own[0] = start[...]

    @pl.when((seq + seg > 0) & jnp.logical_not(follows))
    def _():
        start_copy().start()

    def send_bias(j, _):
        @pl.when(j != seq)
        def _():
            remote(
                bias.at[home], bias.at[home], bias_send_sem.at[j], bias_sem.at[home], j, seg
            ).start()

        return 0

    def send_obs(j, _):
        @pl.when(2 * j != seq)
        def _():
            remote(
                obs.at[home], obs.at[home], obs_send_sem.at[j], obs_sem.at[home], 2 * j, seg
            ).start()

        return 0

    @pl.when(keeps)
    def _():
        for level in range(4):
            usable = (mask_ref[0, level] == 1) & (seq >= 2**level)
            row = jnp.full((8, 128), jnp.where(usable, 0.0, NEG), jnp.float32)
            bias[home, :, 128 * level : 128 * (level + 1)] = row
        lax.fori_loop(0, 16, send_bias, 0)
        own_obs.wait()

        @pl.when(seg >= 6)
        def _():
            lax.fori_loop(0, 8, send_obs, 0)

    row = lax.broadcasted_iota(jnp.int32, (256, 128), 0) % 128
    column = lax.broadcasted_iota(jnp.int32, (256, 128), 1)
    causal[...] = jnp.where(column <= row, 0.0, NEG)
    acc[...] = jnp.zeros_like(acc)

    @pl.when(lane == 0)
    def _():
        k_cross[0] = jnp.zeros_like(k_cross[0])
        v_cross[0] = jnp.zeros_like(v_cross[0])

    @pl.when(follows)
    def _():
        pl.semaphore_wait(token, 1)
        start_copy().start()

    @pl.when(leads)
    def _():
        start_copy().wait_send()
        signal(token, 2 * after + parity, after_seg)

    left = lax.broadcasted_iota(jnp.int32, (128, 128), 1) < 64

    def weight(t, i):
        @pl.when(t == 0)
        def _():
            target = weights[i][1]
            arrived(target, w_sem.at[i])

    def tick(t, _):
        @pl.when((seq + seg > 0) | (t > 0))
        def _():
            arrived(x_own.at[t], own_sem.at[t])

        weight(t, 0)
        normed[...] = rms(rows_of(x_own.at[t]).astype(jnp.float32), gain_ref[...])
        weight(t, 1)
        weight(t, 2)
        for c in range(CHUNKS):
            columns = slice(256 * c, 256 * (c + 1))
            k = jnp.dot(normed[...], wk[:, columns], preferred_element_type=jnp.float32)
            v = jnp.dot(normed[...], wv[:, columns], preferred_element_type=jnp.float32)
            for i in range(2):
                part = slice(128 * i, 128 * (i + 1))
                k_own[t, 2 * c + i] = k[:, part].astype(jnp.bfloat16)
                v_own[t, 2 * c + i] = v[:, part].astype(jnp.bfloat16)

        @pl.when(t + lane < TICKS)
        def _():
            for i, (mine, theirs) in enumerate(((k_own, k_cross), (v_own, v_cross))):
                remote(
                    mine.at[t],
                    theirs.at[t + lane],
                    send_cross_sem.at[i, t],
                    cross_sem.at[i, t + lane],
                    seq,
                    sibling,
                ).start()

        weight(t, 3)
        for c in range(CHUNKS):
            columns = slice(256 * c, 256 * (c + 1))
            q = jnp.dot(normed[...], wq[:, columns], preferred_element_type=jnp.float32) * 0.125
            for i in range(2):
                part = slice(128 * i, 128 * (i + 1))
                q_buf[2 * c + i, 0:128] = jnp.where(left, q[:, part], 0.0).astype(jnp.bfloat16)
                q_buf[2 * c + i, 128:256] = jnp.where(left, 0.0, q[:, part]).astype(jnp.bfloat16)

        @pl.when((t != home) | jnp.logical_not(keeps))
        def _():
            arrived(bias.at[t], bias_sem.at[t])

        @pl.when((lane == 1) | (t > 0))
        def _():
            arrived(k_cross.at[t], cross_sem.at[0, t])
            arrived(v_cross.at[t], cross_sem.at[1, t])

        def attend(p, levels):
            behind = [jnp.maximum(t - offset, 0) for offset in (1, 2, 4)[: levels - 1]]
            count = 128 * levels
            keys = jnp.concatenate(
                [k_own[t, p], k_cross[t, p]] + [k_own[index, p] for index in behind], axis=0
            )
            values = jnp.concatenate(
                [v_own[t, p], v_cross[t, p]] + [v_own[index, p] for index in behind], axis=0
            )
            ones = jnp.ones((128 + count, 128), jnp.bfloat16)
            scores = lax.dot_general(
                q_buf[p], keys, (((1,), (1,)), ((), ())), preferred_element_type=jnp.float32
            )
            scores = jnp.concatenate(
                [scores[:, 0:128] + causal[...], scores[:, 128:] + bias[t, 0:1, 0:count]], axis=1
            )
            peak = jnp.max(scores, axis=-1, keepdims=True)
            expon = jnp.exp(scores - peak).astype(jnp.bfloat16)
            both = jnp.dot(
                expon, jnp.concatenate([values, ones], axis=1), preferred_element_type=jnp.float32
            )
            mixed = both[:, 0:128] / both[:, 128:256]
            ctx[p] = jnp.where(left, mixed[0:128], mixed[128:256]).astype(jnp.bfloat16)

        def attend_all(levels):
            def some(i, _):
                for u in range(UNROLL):
                    attend(UNROLL * i + u, levels)
                return 0

            lax.fori_loop(0, PAIRS // UNROLL, some, 0)

        for levels, low_tick, high_tick in ((1, 0, 1), (2, 1, 2), (3, 2, 4), (4, 4, 8)):

            @pl.when((t >= low_tick) & (t < high_tick))
            def _():
                attend_all(levels)

        weight(t, 4)
        context = jnp.concatenate([ctx[p] for p in range(PAIRS)], axis=1)
        for c in range(CHUNKS):
            columns = slice(256 * c, 256 * (c + 1))
            mixed = jnp.dot(context, wo[:, columns], preferred_element_type=jnp.float32)
            x_out[t, c] = (x_own[t, c].astype(jnp.float32) + mixed).astype(jnp.bfloat16)

            @pl.when(stage < last)
            def _():
                remote(
                    x_out.at[t, c],
                    x_own.at[t, c],
                    send_own_sem.at[t],
                    own_sem.at[t],
                    next_seq,
                    next_seg,
                ).start()

        @pl.when(stage == last)
        def _():
            ended = rms(rows_of(x_out.at[t]).astype(jnp.float32), out_gain_ref[...])
            predicted = jnp.dot(ended, w_read_ref[...], preferred_element_type=jnp.float32)
            block = 2 * t + lane
            pred_send[t] = predicted

            @pl.when((block != seq) | (member != seg))
            def _():
                remote(
                    pred_send.at[t], pred_recv, pred_send_sem.at[t], pred_sem, block, member
                ).start()

            @pl.when((block == seq) & (member == seg))
            def _():
                pred_recv[...] = predicted

            @pl.when(block != seq)
            def _():
                arrived(obs.at[t], obs_sem.at[t])

            errors = predicted - obs[t]
            hours = lax.broadcasted_iota(jnp.int32, (128, 128), 0) + block * 128
            weighting = 1.0 + hours.astype(jnp.float32) * (2.0 / 2047.0)
            squares = weighting * errors * errors
            acc[...] += jnp.sum(squares.reshape(16, 8, 128), axis=0)

        return 0

    lax.fori_loop(0, TICKS, tick, 0)

    def fit_copy(j):
        return remote(
            fit_send, fit_recv.at[lane], fit_send_sem.at[j], fit_sem.at[lane], j, member
        )

    def send_fit(j, _):
        @pl.when((j != seq) | (member != seg))
        def _():
            fit_copy(j).start()

        return 0

    def sent_fit(j, _):
        @pl.when((j != seq) | (member != seg))
        def _():
            fit_copy(j).wait_send()

        return 0

    @pl.when(final)
    def _():
        fit_send[...] = acc[...]
        lax.fori_loop(0, 16, send_fit, 0)

        @pl.when(member == seg)
        def _():
            fit_recv[lane] = acc[...]

    def sent_tick(t, _):
        @pl.when(stage < last)
        def _():
            arrived(x_out.at[t], send_own_sem.at[t])

        @pl.when(t + lane < TICKS)
        def _():
            arrived(k_own.at[t], send_cross_sem.at[0, t])
            arrived(v_own.at[t], send_cross_sem.at[1, t])

        @pl.when(final & ((2 * t + lane != seq) | (member != seg)))
        def _():
            arrived(pred_send.at[t], pred_send_sem.at[t])

        @pl.when(keeps & (seg >= 6) & (2 * t != seq))
        def _():
            arrived(obs.at[home], obs_send_sem.at[t])

        return 0

    def sent_bias(j, _):
        @pl.when(j != seq)
        def _():
            arrived(bias.at[home], bias_send_sem.at[j])

        return 0

    lax.fori_loop(0, TICKS, sent_tick, 0)

    @pl.when(keeps)
    def _():
        lax.fori_loop(0, 16, sent_bias, 0)

    @pl.when((seq + seg > 0) & jnp.logical_not(leads))
    def _():
        start_copy().wait_send()

    @pl.when(owner)
    def _():
        for i, (source, target) in enumerate(weights):
            arrived(target, w_send_sem.at[i])

    @pl.when(final)
    def _():
        lax.fori_loop(0, 16, sent_fit, 0)

    @pl.when((seq != 2 * seg) | (seg != 6))
    def _():
        arrived(pred_recv, pred_sem)

    for source in range(2):

        @pl.when((seq != 2 * seg) | (seg != 6 + source))
        def _():
            arrived(fit_recv.at[source], fit_sem.at[source])

    pred_out[...] = pred_recv[...]
    total = jnp.sum(fit_recv[0] + fit_recv[1])
    fit_out[0] = -total / (2048.0 * 128.0)


def per_device(
    base_state,
    forcing,
    theta_base,
    perturb,
    order,
    w_force,
    attn_gain,
    w_query,
    w_key,
    w_value,
    w_out,
    block_mask,
    out_gain,
    w_read,
    observed,
):
    bf16, f32, i32 = jnp.bfloat16, jnp.float32, jnp.int32
    dma = pltpu.SemaphoreType.DMA
    predictions, fitness = pl.pallas_call(
        kernel,
        out_shape=(
            jax.ShapeDtypeStruct((128, 128), f32),
            jax.ShapeDtypeStruct((1,), f32),
        ),
        in_specs=[pl.BlockSpec(memory_space=pl.ANY)] * 15,
        out_specs=(
            pl.BlockSpec(memory_space=pltpu.VMEM),
            pl.BlockSpec(memory_space=pltpu.SMEM),
        ),
        scratch_shapes=[
            pltpu.VMEM((128, 1024), bf16),
            pltpu.VMEM((64, 128), f32),
            pltpu.VMEM((1, 64), f32),
            pltpu.VMEM((32, 64), f32),
            pltpu.SMEM((32,), i32),
            pltpu.VMEM((64, 1024), bf16),
            pltpu.VMEM((1, 1024), f32),
            pltpu.SMEM((1, 4), i32),
            pltpu.VMEM((1, 1024), f32),
            pltpu.VMEM((1024, 128), bf16),
            pltpu.VMEM((1024, 1024), bf16),
            pltpu.VMEM((1024, 1024), bf16),
            pltpu.VMEM((1024, 1024), bf16),
            pltpu.VMEM((1024, 1024), bf16),
            pltpu.VMEM((TICKS, CHUNKS, 128, 256), bf16),
            pltpu.VMEM((TICKS, CHUNKS, 128, 256), bf16),
            pltpu.VMEM((CHUNKS, 128, 256), bf16),
            pltpu.VMEM((128, 1024), bf16),
            pltpu.VMEM((PAIRS, 256, 128), bf16),
            pltpu.VMEM((TICKS, PAIRS, 128, 128), bf16),
            pltpu.VMEM((TICKS, PAIRS, 128, 128), bf16),
            pltpu.VMEM((TICKS, PAIRS, 128, 128), bf16),
            pltpu.VMEM((TICKS, PAIRS, 128, 128), bf16),
            pltpu.VMEM((PAIRS, 128, 128), bf16),
            pltpu.VMEM((256, 128), f32),
            pltpu.VMEM((TICKS, 8, 512), f32),
            pltpu.VMEM((TICKS, 128, 128), f32),
            pltpu.VMEM((TICKS, 128, 128), f32),
            pltpu.VMEM((128, 128), f32),
            pltpu.VMEM((8, 128), f32),
            pltpu.VMEM((8, 128), f32),
            pltpu.VMEM((2, 8, 128), f32),
            dma((10,)),
            dma((5,)),
            dma((5,)),
            dma((TICKS,)),
            dma((TICKS,)),
            dma((2, TICKS)),
            dma((2, TICKS)),
            dma,
            dma((TICKS,)),
            dma((16,)),
            dma((TICKS,)),
            dma((8,)),
            dma,
            dma((TICKS,)),
            dma((2,)),
            dma((16,)),
            pltpu.SemaphoreType.REGULAR,
        ],
        compiler_params=pltpu.CompilerParams(
            has_side_effects=True, collective_id=0, vmem_limit_bytes=60 * 1024 * 1024
        ),
    )(
        base_state,
        forcing.T,
        theta_base.reshape(1, -1),
        perturb,
        order,
        w_force,
        attn_gain,
        w_query,
        w_key,
        w_value,
        w_out,
        block_mask,
        out_gain.reshape(1, -1),
        w_read,
        observed,
    )
    return predictions[None], fitness


def solution(mesh):
    placed = (
        P("seq", None),
        P("seq", None),
        P(),
        P(),
        P(),
        P(),
        P("segment", None),
        P("segment", None, None),
        P("segment", None, None),
        P("segment", None, None),
        P("segment", None, None),
        P("seq", None),
        P(),
        P(),
        P("seq", None),
    )
    return jax.shard_map(
        per_device,
        mesh=mesh,
        in_specs=placed,
        out_specs=(P("segment", "seq", None), P("segment")),
        check_vma=False,
    )
```

```python
import jax
import jax.numpy as jnp
from jax import lax
from jax.experimental import pallas as pl
from jax.experimental.pallas import tpu as pltpu
from jax.sharding import PartitionSpec as P

TICKS = 8
PAIRS = 8
CHUNKS = 4
UNROLL = 4
NEG = -1e30


def rms(values, gain):
    meansq = jnp.mean(values * values, axis=-1, keepdims=True) + 1e-05
    return (values * lax.rsqrt(meansq) * gain).astype(jnp.bfloat16)


def rows_of(ref):
    return jnp.concatenate([ref[c] for c in range(CHUNKS)], axis=1)


def kernel(
    base_hbm,
    forcing_hbm,
    theta_hbm,
    perturb_hbm,
    order_hbm,
    w_force_hbm,
    gain_hbm,
    wq_hbm,
    wk_hbm,
    wv_hbm,
    wo_hbm,
    mask_hbm,
    out_gain_hbm,
    w_read_hbm,
    observed_hbm,
    pred_out,
    fit_out,
    base_ref,
    forcing_ref,
    theta_ref,
    perturb_ref,
    order_ref,
    w_force_ref,
    gain_ref,
    mask_ref,
    out_gain_ref,
    w_read_ref,
    wq,
    wk,
    wv,
    wo,
    x_own,
    x_cross,
    x_out,
    starts,
    normed,
    q_buf,
    k_own,
    v_own,
    k_cross,
    v_cross,
    ctx,
    part,
    peaks,
    causal,
    bias,
    obs,
    pred_send,
    pred_recv,
    acc,
    fit_send,
    fit_recv,
    w_sem,
    own_sem,
    cross_sem,
    send_own_sem,
    send_cross_sem,
    start_sem,
    bias_sem,
    bias_send_sem,
    obs_sem,
    obs_send_sem,
    pred_sem,
    pred_send_sem,
    fit_sem,
    fit_send_sem,
    token,
):
    seq = lax.axis_index("seq")
    seg = lax.axis_index("segment")
    lane = seq % 2
    member = seq // 2
    home = seq // 2
    other = seq + 1 - 2 * lane
    last = 7

    def remote(src, dst, send, recv, to_seq, to_seg):
        return pltpu.make_async_remote_copy(
            src_ref=src,
            dst_ref=dst,
            send_sem=send,
            recv_sem=recv,
            device_id={"seq": to_seq, "segment": to_seg},
            device_id_type=pl.DeviceIdType.MESH,
        )

    first = [
        (base_hbm, base_ref),
        (forcing_hbm, forcing_ref),
        (theta_hbm, theta_ref),
        (perturb_hbm, perturb_ref),
        (order_hbm, order_ref),
        (w_force_hbm, w_force_ref),
    ]
    second = [
        (mask_hbm, mask_ref),
        (gain_hbm, gain_ref),
        (wq_hbm.at[0], wq),
        (wk_hbm.at[0], wk),
        (wv_hbm.at[0], wv),
        (wo_hbm.at[0], wo),
        (out_gain_hbm, out_gain_ref),
        (w_read_hbm, w_read_ref),
        (observed_hbm, obs.at[home]),
    ]
    def signal(sem, to_seq, to_seg):
        pl.semaphore_signal(
            sem,
            inc=1,
            device_id={"seq": to_seq, "segment": to_seg},
            device_id_type=pl.DeviceIdType.MESH,
        )

    def arrived(ref, sem):
        pltpu.make_async_copy(ref, ref, sem).wait()

    loads = [
        pltpu.make_async_copy(source, target, w_sem.at[i])
        for i, (source, target) in enumerate(first + second)
    ]
    for load in loads:
        load.start()

    plane = seg // 2
    core = seg % 2
    slot = 2 * ((plane + 8 - home) % 4) + core
    before = home - 3 + plane // 3
    after = home + 3 - (plane % 2) * (1 - plane // 3)
    follows = (plane > 0) & (before >= 0)
    leads = (plane > 0) & (after < 8)

    barrier = pltpu.get_barrier_semaphore()
    even = 1 - seg % 2
    ends = seg // last

    @pl.when(seg > 0)
    def _():
        signal(barrier, seq, seg - 1)

    signal(barrier, other, seg - seg % 2)

    def greet(t, _):
        source = 2 * t + lane

        @pl.when(source != seq)
        def _():
            signal(barrier, source, seg)

        @pl.when((seg == 0) & ((home > 0) | (t > 0)))
        def _():
            signal(barrier, source, 2 * ((member // 2 + t) % 4) + member % 2)

        return 0

    lax.fori_loop(0, TICKS, greet, 0)

    @pl.when(follows)
    def _():
        signal(barrier, 2 * before + lane, 2 * (plane % 3 + 1) + core)

    for source in range(2):

        @pl.when((seq != 2 * seg + source) | (seg != last))
        def _():
            signal(barrier, 2 * seg + source, last)

    expected = 9 - ends + 2 * even
    expected += ((plane + 2) // 3) * (1 - after // 8)
    expected += ends * (16 - member // last)
    expected -= 1 - (seg + home + 13) // 14
    pl.semaphore_wait(barrier, expected)

    for load in loads[: len(first)]:
        load.wait()

    def start_copy():
        return remote(starts, x_own.at[home], start_sem, own_sem.at[home, 0], 2 * slot + lane, 0)

    theta = theta_ref[...] + 0.5 * perturb_ref[pl.ds(order_ref[slot], 1), :]
    drive = forcing_ref[...].T * theta
    high = drive.astype(jnp.bfloat16)
    rest = drive - high.astype(jnp.float32)
    middle = rest.astype(jnp.bfloat16)
    low = (rest - middle.astype(jnp.float32)).astype(jnp.bfloat16)
    for c in range(CHUNKS):
        columns = slice(256 * c, 256 * (c + 1))
        w = w_force_ref[:, columns]
        lifted = jnp.dot(low, w, preferred_element_type=jnp.float32)
        lifted += jnp.dot(middle, w, preferred_element_type=jnp.float32)
        lifted += jnp.dot(high, w, preferred_element_type=jnp.float32)
        starts[c] = (base_ref[:, columns].astype(jnp.float32) + lifted).astype(jnp.bfloat16)

    @pl.when((seg == 0) & (home == 0))
    def _():
        x_own[0] = starts[...]

    @pl.when((seg + home > 0) & jnp.logical_not(follows))
    def _():
        start_copy().start()

    for load in loads[len(first) :]:
        load.wait()

    for level in range(4):
        usable = (mask_ref[0, level] == 1) & (seq >= 2**level)
        row = jnp.full((8, 128), jnp.where(usable, 0.0, NEG), jnp.float32)
        bias[home, :, 128 * level : 128 * (level + 1)] = row

    def send_bias(j, _):
        target = 2 * j + lane

        @pl.when(target != seq)
        def _():
            remote(
                bias.at[home], bias.at[home], bias_send_sem.at[j], bias_sem.at[home], target, seg
            ).start()

        return 0

    lax.fori_loop(0, 8, send_bias, 0)

    def send_obs(j, _):
        target = 2 * j + lane

        @pl.when(target != seq)
        def _():
            remote(
                obs.at[home], obs.at[home], obs_send_sem.at[j], obs_sem.at[home], target, last
            ).start()

        return 0

    @pl.when(seg == last)
    def _():
        lax.fori_loop(0, 8, send_obs, 0)

    row = lax.broadcasted_iota(jnp.int32, (256, 128), 0) % 128
    column = lax.broadcasted_iota(jnp.int32, (256, 128), 1)
    causal[...] = jnp.where(column <= row, 0.0, NEG)
    acc[...] = jnp.zeros_like(acc)

    @pl.when(lane == 0)
    def _():
        x_cross[0] = jnp.zeros_like(x_cross[0])

    left = lax.broadcasted_iota(jnp.int32, (128, 128), 1) < 64

    def tick(t, _):
        for c in range(CHUNKS):

            @pl.when((seg == 0) & (t + home > 0) & (c == 0))
            def _():
                arrived(x_own.at[t], own_sem.at[t, 0])

            @pl.when(seg > 0)
            def _():
                arrived(x_own.at[t, c], own_sem.at[t, c])

            @pl.when((seg % 2 == 0) & (t + lane < TICKS))
            def _():
                remote(
                    x_own.at[t, c],
                    x_cross.at[t + lane, c],
                    send_cross_sem.at[t],
                    cross_sem.at[t + lane],
                    other,
                    seg,
                ).start()

        x = rows_of(x_own.at[t]).astype(jnp.float32)
        gain = gain_ref[...]
        normed[0:128] = rms(x, gain)

        for c in range(CHUNKS):
            columns = slice(256 * c, 256 * (c + 1))
            q = jnp.dot(normed[0:128], wq[:, columns], preferred_element_type=jnp.float32) * 0.125
            k = jnp.dot(normed[0:128], wk[:, columns], preferred_element_type=jnp.float32)
            v = jnp.dot(normed[0:128], wv[:, columns], preferred_element_type=jnp.float32)
            for i in range(2):
                p = 2 * c + i
                half = slice(128 * i, 128 * (i + 1))
                q_buf[p, 0:128] = jnp.where(left, q[:, half], 0.0).astype(jnp.bfloat16)
                q_buf[p, 128:256] = jnp.where(left, 0.0, q[:, half]).astype(jnp.bfloat16)
                k_own[t, p] = k[:, half].astype(jnp.bfloat16)
                v_own[t, p] = v[:, half].astype(jnp.bfloat16)

        @pl.when(t != home)
        def _():
            arrived(bias.at[t], bias_sem.at[t])

        def scores_of(p, keys):
            return lax.dot_general(
                q_buf[p], keys, (((1,), (1,)), ((), ())), preferred_element_type=jnp.float32
            )

        def mix(expon, values):
            ones = jnp.ones((values.shape[0], 128), jnp.bfloat16)
            return jnp.dot(
                expon, jnp.concatenate([values, ones], axis=1), preferred_element_type=jnp.float32
            )

        def all_pairs(unroll, attend):
            def some(i, _):
                for u in range(unroll):
                    attend(unroll * i + u)
                return 0

            lax.fori_loop(0, PAIRS // unroll, some, 0)

        def attend_own(p, levels):
            behind = [t - offset for offset in (1, 2, 4)[: levels - 1]]
            keys = jnp.concatenate([k_own[t, p]] + [k_own[index, p] for index in behind], axis=0)
            values = jnp.concatenate([v_own[t, p]] + [v_own[index, p] for index in behind], axis=0)
            scores = scores_of(p, keys)
            seen = [scores[:, 0:128] + causal[...]]
            if levels > 1:
                seen.append(scores[:, 128:] + bias[t, 0:1, 128 : 128 * levels])
            scores = jnp.concatenate(seen, axis=1)
            peak = jnp.max(scores, axis=-1, keepdims=True)
            part[p] = mix(jnp.exp(scores - peak).astype(jnp.bfloat16), values)
            peaks[p] = jnp.broadcast_to(peak, (256, 128))

        for levels, low_tick, high_tick in ((1, 0, 1), (2, 1, 2), (3, 2, 4), (4, 4, 8)):

            @pl.when((t >= low_tick) & (t < high_tick))
            def _():
                all_pairs(UNROLL, lambda p: attend_own(p, levels))

        @pl.when((lane == 1) | (t > 0))
        def _():
            arrived(x_cross.at[t], cross_sem.at[t])

        normed[128:256] = rms(rows_of(x_cross.at[t]).astype(jnp.float32), gain)

        for c in range(CHUNKS):
            columns = slice(256 * c, 256 * (c + 1))
            k = jnp.dot(normed[128:256], wk[:, columns], preferred_element_type=jnp.float32)
            v = jnp.dot(normed[128:256], wv[:, columns], preferred_element_type=jnp.float32)
            for i in range(2):
                half = slice(128 * i, 128 * (i + 1))
                k_cross[2 * c + i] = k[:, half].astype(jnp.bfloat16)
                v_cross[2 * c + i] = v[:, half].astype(jnp.bfloat16)

        def attend_cross(p):
            scores = scores_of(p, k_cross[p]) + bias[t, 0:1, 0:128]
            before = peaks[p]
            peak = jnp.maximum(before, jnp.max(scores, axis=-1, keepdims=True))
            scale = jnp.exp(before - peak)
            added = mix(jnp.exp(scores - peak).astype(jnp.bfloat16), v_cross[p])
            kept = part[p]
            over = kept[:, 0:128] * scale + added[:, 0:128]
            under = kept[:, 128:256] * scale + added[:, 128:256]
            mixed = over / under
            ctx[p] = jnp.where(left, mixed[0:128], mixed[128:256]).astype(jnp.bfloat16)

        all_pairs(PAIRS, attend_cross)

        context = jnp.concatenate([ctx[p] for p in range(PAIRS)], axis=1)
        for c in range(CHUNKS):
            columns = slice(256 * c, 256 * (c + 1))
            mixed = jnp.dot(context, wo[:, columns], preferred_element_type=jnp.float32)
            x_out[t, c] = (x_own[t, c].astype(jnp.float32) + mixed).astype(jnp.bfloat16)

            @pl.when(seg < last)
            def _():
                remote(
                    x_out.at[t, c],
                    x_own.at[t, c],
                    send_own_sem.at[t],
                    own_sem.at[t, c],
                    seq,
                    seg + 1,
                ).start()

            @pl.when((seg % 2 == 0) & (t + lane < TICKS))
            def _():
                remote(
                    x_out.at[t, c],
                    x_cross.at[t + lane, c],
                    send_cross_sem.at[t + TICKS],
                    cross_sem.at[t + lane],
                    other,
                    seg + 1,
                ).start()

        @pl.when(seg == last)
        def _():
            final = rms(rows_of(x_out.at[t]).astype(jnp.float32), out_gain_ref[...])
            predicted = jnp.dot(final, w_read_ref[...], preferred_element_type=jnp.float32)
            block = 2 * t + lane
            pred_send[t] = predicted

            @pl.when((block != seq) | (member != last))
            def _():
                remote(
                    pred_send.at[t], pred_recv, pred_send_sem.at[t], pred_sem, block, member
                ).start()

            @pl.when((block == seq) & (member == last))
            def _():
                pred_recv[...] = predicted

            @pl.when(t != home)
            def _():
                pltpu.make_async_copy(obs.at[t], obs.at[t], obs_sem.at[t]).wait()

            errors = predicted - obs[t]
            hours = lax.broadcasted_iota(jnp.int32, (128, 128), 0) + block * 128
            weight = 1.0 + hours.astype(jnp.float32) * (2.0 / 2047.0)
            squares = weight * errors * errors
            acc[...] += jnp.sum(squares.reshape(16, 8, 128), axis=0)

        return 0

    @pl.when(follows)
    def _():
        pl.semaphore_wait(token, 1)
        start_copy().start()

    @pl.when(leads)
    def _():
        start_copy().wait_send()
        signal(token, 2 * after + lane, 2 * ((plane + 1) % 3 + 1) + core)

    lax.fori_loop(0, TICKS, tick, 0)

    def send_fit(j, _):
        @pl.when((j != seq) | (member != last))
        def _():
            remote(
                fit_send, fit_recv.at[lane], fit_send_sem.at[j], fit_sem.at[lane], j, member
            ).start()

        return 0

    def sent_fit(j, _):
        @pl.when((j != seq) | (member != last))
        def _():
            remote(
                fit_send, fit_recv.at[lane], fit_send_sem.at[j], fit_sem.at[lane], j, member
            ).wait_send()

        return 0

    @pl.when(seg == last)
    def _():
        fit_send[...] = acc[...]
        lax.fori_loop(0, 16, send_fit, 0)

        @pl.when(member == last)
        def _():
            fit_recv[lane] = acc[...]

    def sent_tick(t, _):
        @pl.when(seg < last)
        def _():
            pltpu.make_async_copy(x_out.at[t], x_out.at[t], send_own_sem.at[t]).wait()

        @pl.when((seg % 2 == 0) & (t + lane < TICKS))
        def _():
            pltpu.make_async_copy(x_out.at[t], x_out.at[t], send_cross_sem.at[t + TICKS]).wait()
            pltpu.make_async_copy(x_own.at[t], x_own.at[t], send_cross_sem.at[t]).wait()

        @pl.when(2 * t + lane != seq)
        def _():
            pltpu.make_async_copy(bias.at[home], bias.at[home], bias_send_sem.at[t]).wait()

        @pl.when(seg == last)
        def _():
            @pl.when(2 * t + lane != seq)
            def _():
                pltpu.make_async_copy(obs.at[home], obs.at[home], obs_send_sem.at[t]).wait()

            @pl.when((2 * t + lane != seq) | (member != last))
            def _():
                pltpu.make_async_copy(pred_send.at[t], pred_send.at[t], pred_send_sem.at[t]).wait()

        return 0

    lax.fori_loop(0, TICKS, sent_tick, 0)

    @pl.when((seg + home > 0) & jnp.logical_not(leads))
    def _():
        start_copy().wait_send()

    @pl.when(seg == last)
    def _():
        lax.fori_loop(0, 16, sent_fit, 0)

    @pl.when((seg != last) | (member != last))
    def _():
        pltpu.make_async_copy(pred_recv, pred_recv, pred_sem).wait()

    for source in range(2):

        @pl.when((seg != last) | (seq != 14 + source))
        def _():
            pltpu.make_async_copy(fit_recv.at[source], fit_recv.at[source], fit_sem.at[source]).wait()

    pred_out[...] = pred_recv[...]
    total = jnp.sum(fit_recv[0] + fit_recv[1])
    fit_out[0] = -total / (2048.0 * 128.0)


def per_device(
    base_state,
    forcing,
    theta_base,
    perturb,
    order,
    w_force,
    attn_gain,
    w_query,
    w_key,
    w_value,
    w_out,
    block_mask,
    out_gain,
    w_read,
    observed,
):
    vmem = pl.BlockSpec(memory_space=pltpu.VMEM)
    smem = pl.BlockSpec(memory_space=pltpu.SMEM)
    hbm = pl.BlockSpec(memory_space=pl.ANY)
    bf16, f32 = jnp.bfloat16, jnp.float32
    dma = pltpu.SemaphoreType.DMA
    predictions, fitness = pl.pallas_call(
        kernel,
        out_shape=(
            jax.ShapeDtypeStruct((128, 128), f32),
            jax.ShapeDtypeStruct((1,), f32),
        ),
        in_specs=[hbm] * 15,
        out_specs=(vmem, smem),
        scratch_shapes=[
            pltpu.VMEM((128, 1024), bf16),
            pltpu.VMEM((64, 128), f32),
            pltpu.VMEM((1, 64), f32),
            pltpu.VMEM((32, 64), f32),
            pltpu.SMEM((32,), jnp.int32),
            pltpu.VMEM((64, 1024), bf16),
            pltpu.VMEM((1, 1024), f32),
            pltpu.SMEM((1, 4), jnp.int32),
            pltpu.VMEM((1, 1024), f32),
            pltpu.VMEM((1024, 128), bf16),
            pltpu.VMEM((1024, 1024), bf16),
            pltpu.VMEM((1024, 1024), bf16),
            pltpu.VMEM((1024, 1024), bf16),
            pltpu.VMEM((1024, 1024), bf16),
            pltpu.VMEM((TICKS, CHUNKS, 128, 256), bf16),
            pltpu.VMEM((TICKS, CHUNKS, 128, 256), bf16),
            pltpu.VMEM((TICKS, CHUNKS, 128, 256), bf16),
            pltpu.VMEM((CHUNKS, 128, 256), bf16),
            pltpu.VMEM((256, 1024), bf16),
            pltpu.VMEM((PAIRS, 256, 128), bf16),
            pltpu.VMEM((TICKS, PAIRS, 128, 128), bf16),
            pltpu.VMEM((TICKS, PAIRS, 128, 128), bf16),
            pltpu.VMEM((PAIRS, 128, 128), bf16),
            pltpu.VMEM((PAIRS, 128, 128), bf16),
            pltpu.VMEM((PAIRS, 128, 128), bf16),
            pltpu.VMEM((PAIRS, 256, 256), f32),
            pltpu.VMEM((PAIRS, 256, 128), f32),
            pltpu.VMEM((256, 128), f32),
            pltpu.VMEM((TICKS, 8, 512), f32),
            pltpu.VMEM((TICKS, 128, 128), f32),
            pltpu.VMEM((TICKS, 128, 128), f32),
            pltpu.VMEM((128, 128), f32),
            pltpu.VMEM((8, 128), f32),
            pltpu.VMEM((8, 128), f32),
            pltpu.VMEM((2, 8, 128), f32),
            dma((15,)),
            dma((TICKS, CHUNKS)),
            dma((TICKS,)),
            dma((TICKS,)),
            dma((2 * TICKS,)),
            dma,
            dma((TICKS,)),
            dma((8,)),
            dma((TICKS,)),
            dma((8,)),
            dma,
            dma((TICKS,)),
            dma((2,)),
            dma((16,)),
            pltpu.SemaphoreType.REGULAR,
        ],
        compiler_params=pltpu.CompilerParams(
            has_side_effects=True, collective_id=0, vmem_limit_bytes=60 * 1024 * 1024
        ),
    )(
        base_state,
        forcing.T,
        theta_base.reshape(1, -1),
        perturb,
        order,
        w_force,
        attn_gain,
        w_query,
        w_key,
        w_value,
        w_out,
        block_mask,
        out_gain.reshape(1, -1),
        w_read,
        observed,
    )
    return predictions[None], fitness


def solution(mesh):
    placed = (
        P("seq", None),
        P("seq", None),
        P(),
        P(),
        P(),
        P(),
        P("segment", None),
        P("segment", None, None),
        P("segment", None, None),
        P("segment", None, None),
        P("segment", None, None),
        P("seq", None),
        P(),
        P(),
        P("seq", None),
    )
    return jax.shard_map(
        per_device,
        mesh=mesh,
        in_specs=placed,
        out_specs=(P("segment", "seq", None), P("segment")),
        check_vma=False,
    )
```

```python
import jax
import jax.numpy as jnp
from jax import lax
from jax.experimental import pallas as pl
from jax.experimental.pallas import tpu as pltpu
from jax.sharding import PartitionSpec as P

TICKS = 8
PAIRS = 8
CHUNKS = 4
NEG = -1e30


def rms(values, gain):
    meansq = jnp.mean(values * values, axis=-1, keepdims=True) + 1e-05
    return (values * lax.rsqrt(meansq) * gain).astype(jnp.bfloat16)


def rows_of(ref):
    return jnp.concatenate([ref[c] for c in range(CHUNKS)], axis=1)


def kernel(
    base_hbm,
    forcing_hbm,
    theta_hbm,
    perturb_hbm,
    order_hbm,
    w_force_hbm,
    gain_hbm,
    wq_hbm,
    wk_hbm,
    wv_hbm,
    wo_hbm,
    mask_hbm,
    out_gain_hbm,
    w_read_hbm,
    observed_hbm,
    pred_out,
    fit_out,
    base_ref,
    forcing_ref,
    theta_ref,
    perturb_ref,
    order_ref,
    w_force_ref,
    gain_ref,
    mask_ref,
    out_gain_ref,
    w_read_ref,
    wq,
    wk,
    wv,
    wo,
    x_own,
    x_cross,
    x_out,
    starts,
    normed,
    q_buf,
    k_own,
    v_own,
    k_cross,
    v_cross,
    ctx,
    part,
    peaks,
    causal,
    bias,
    obs,
    pred_send,
    pred_recv,
    acc,
    fit_send,
    fit_recv,
    w_sem,
    own_sem,
    cross_sem,
    send_own_sem,
    send_cross_sem,
    start_sem,
    bias_sem,
    bias_send_sem,
    obs_sem,
    obs_send_sem,
    pred_sem,
    pred_send_sem,
    fit_sem,
    fit_send_sem,
    token,
):
    seq = lax.axis_index("seq")
    seg = lax.axis_index("segment")
    lane = seq % 2
    member = seq // 2
    home = seq // 2
    other = seq + 1 - 2 * lane
    last = 7

    def remote(src, dst, send, recv, to_seq, to_seg):
        return pltpu.make_async_remote_copy(
            src_ref=src,
            dst_ref=dst,
            send_sem=send,
            recv_sem=recv,
            device_id={"seq": to_seq, "segment": to_seg},
            device_id_type=pl.DeviceIdType.MESH,
        )

    first = [
        (base_hbm, base_ref),
        (forcing_hbm, forcing_ref),
        (theta_hbm, theta_ref),
        (perturb_hbm, perturb_ref),
        (order_hbm, order_ref),
        (w_force_hbm, w_force_ref),
    ]
    second = [
        (mask_hbm, mask_ref),
        (gain_hbm, gain_ref),
        (wq_hbm.at[0], wq),
        (wk_hbm.at[0], wk),
        (wv_hbm.at[0], wv),
        (wo_hbm.at[0], wo),
        (out_gain_hbm, out_gain_ref),
        (w_read_hbm, w_read_ref),
        (observed_hbm, obs.at[home]),
    ]
    def signal(sem, to_seq, to_seg):
        pl.semaphore_signal(
            sem,
            inc=1,
            device_id={"seq": to_seq, "segment": to_seg},
            device_id_type=pl.DeviceIdType.MESH,
        )

    def arrived(ref, sem):
        pltpu.make_async_copy(ref, ref, sem).wait()

    loads = [
        pltpu.make_async_copy(source, target, w_sem.at[i])
        for i, (source, target) in enumerate(first + second)
    ]
    for load in loads:
        load.start()

    plane = seg // 2
    core = seg % 2
    slot = 2 * ((plane + 8 - home) % 4) + core
    before = home - 3 + plane // 3
    after = home + 3 - (plane % 2) * (1 - plane // 3)
    follows = (plane > 0) & (before >= 0)
    leads = (plane > 0) & (after < 8)

    barrier = pltpu.get_barrier_semaphore()
    ends = seg // last

    @pl.when(seg > 0)
    def _():
        signal(barrier, seq, seg - 1)

    signal(barrier, other, seg)

    def greet(t, _):
        source = 2 * t + lane

        @pl.when(source != seq)
        def _():
            signal(barrier, source, seg)

        @pl.when((seg == 0) & ((home > 0) | (t > 0)))
        def _():
            signal(barrier, source, 2 * ((member // 2 + t) % 4) + member % 2)

        return 0

    lax.fori_loop(0, TICKS, greet, 0)

    @pl.when(follows)
    def _():
        signal(barrier, 2 * before + lane, 2 * (plane % 3 + 1) + core)

    for source in range(2):

        @pl.when((seq != 2 * seg + source) | (seg != last))
        def _():
            signal(barrier, 2 * seg + source, last)

    expected = 10 - ends
    expected += ((plane + 2) // 3) * (1 - after // 8)
    expected += ends * (16 - member // last)
    expected -= 1 - (seg + home + 13) // 14
    for load in loads[: len(first)]:
        load.wait()

    def start_copy():
        return remote(starts, x_own.at[home], start_sem, own_sem.at[home, 0], 2 * slot + lane, 0)

    theta = theta_ref[...] + 0.5 * perturb_ref[pl.ds(order_ref[slot], 1), :]
    drive = forcing_ref[...].T * theta
    high = drive.astype(jnp.bfloat16)
    rest = drive - high.astype(jnp.float32)
    middle = rest.astype(jnp.bfloat16)
    low = (rest - middle.astype(jnp.float32)).astype(jnp.bfloat16)
    for c in range(CHUNKS):
        columns = slice(256 * c, 256 * (c + 1))
        w = w_force_ref[:, columns]
        lifted = jnp.dot(low, w, preferred_element_type=jnp.float32)
        lifted += jnp.dot(middle, w, preferred_element_type=jnp.float32)
        lifted += jnp.dot(high, w, preferred_element_type=jnp.float32)
        starts[c] = (base_ref[:, columns].astype(jnp.float32) + lifted).astype(jnp.bfloat16)

    @pl.when((seg == 0) & (home == 0))
    def _():
        x_own[0] = starts[...]

    pl.semaphore_wait(barrier, expected)

    @pl.when((seg + home > 0) & jnp.logical_not(follows))
    def _():
        start_copy().start()

    for load in loads[len(first) :]:
        load.wait()

    for level in range(4):
        usable = (mask_ref[0, level] == 1) & (seq >= 2**level)
        row = jnp.full((8, 128), jnp.where(usable, 0.0, NEG), jnp.float32)
        bias[home, :, 128 * level : 128 * (level + 1)] = row

    def send_bias(j, _):
        target = 2 * j + lane

        @pl.when(target != seq)
        def _():
            remote(
                bias.at[home], bias.at[home], bias_send_sem.at[j], bias_sem.at[home], target, seg
            ).start()

        return 0

    lax.fori_loop(0, 8, send_bias, 0)

    def send_obs(j, _):
        target = 2 * j + lane

        @pl.when(target != seq)
        def _():
            remote(
                obs.at[home], obs.at[home], obs_send_sem.at[j], obs_sem.at[home], target, last
            ).start()

        return 0

    @pl.when(seg == last)
    def _():
        lax.fori_loop(0, 8, send_obs, 0)

    row = lax.broadcasted_iota(jnp.int32, (256, 128), 0) % 128
    column = lax.broadcasted_iota(jnp.int32, (256, 128), 1)
    causal[...] = jnp.where(column <= row, 0.0, NEG)
    acc[...] = jnp.zeros_like(acc)

    @pl.when(lane == 0)
    def _():
        x_cross[0] = jnp.zeros_like(x_cross[0])

    left = lax.broadcasted_iota(jnp.int32, (128, 128), 1) < 64

    def tick(t, _):
        for c in range(CHUNKS):

            @pl.when((seg == 0) & (t + home > 0) & (c == 0))
            def _():
                arrived(x_own.at[t], own_sem.at[t, 0])

            @pl.when(seg > 0)
            def _():
                arrived(x_own.at[t, c], own_sem.at[t, c])

            @pl.when(t + lane < TICKS)
            def _():
                remote(
                    x_own.at[t, c],
                    x_cross.at[t + lane, c],
                    send_cross_sem.at[t],
                    cross_sem.at[t + lane],
                    other,
                    seg,
                ).start()

        @pl.when(t != home)
        def _():
            arrived(bias.at[t], bias_sem.at[t])

        gain = gain_ref[...]

        def scores_of(p, keys):
            return lax.dot_general(
                q_buf[p], keys, (((1,), (1,)), ((), ())), preferred_element_type=jnp.float32
            )

        def mix(expon, values):
            ones = jnp.ones((values.shape[0], 128), jnp.bfloat16)
            return jnp.dot(
                expon, jnp.concatenate([values, ones], axis=1), preferred_element_type=jnp.float32
            )

        def both(pair):
            return jnp.where(left, pair[0:128], pair[128:256])

        def own_part(levels):
            normed[0:128] = rms(rows_of(x_own.at[t]).astype(jnp.float32), gain)
            for c in range(CHUNKS):
                columns = slice(256 * c, 256 * (c + 1))
                mine = normed[0:128]
                q = jnp.dot(mine, wq[:, columns], preferred_element_type=jnp.float32) * 0.125
                k = jnp.dot(mine, wk[:, columns], preferred_element_type=jnp.float32)
                v = jnp.dot(mine, wv[:, columns], preferred_element_type=jnp.float32)
                for i in range(2):
                    p = 2 * c + i
                    half = slice(128 * i, 128 * (i + 1))
                    q_buf[p, 0:128] = jnp.where(left, q[:, half], 0.0).astype(jnp.bfloat16)
                    q_buf[p, 128:256] = jnp.where(left, 0.0, q[:, half]).astype(jnp.bfloat16)
                    k_own[t, p] = k[:, half].astype(jnp.bfloat16)
                    v_own[t, p] = v[:, half].astype(jnp.bfloat16)
            behind = [jnp.maximum(t - offset, 0) for offset in (1, 2, 4)[: levels - 1]]
            for p in range(PAIRS):
                keys = jnp.concatenate([k_own[t, p]] + [k_own[index, p] for index in behind], axis=0)
                values = jnp.concatenate(
                    [v_own[t, p]] + [v_own[index, p] for index in behind], axis=0
                )
                scores = scores_of(p, keys)
                scores = jnp.concatenate(
                    [
                        scores[:, 0:128] + causal[...],
                        scores[:, 128:] + bias[t, 0:1, 128 : 128 * levels],
                    ],
                    axis=1,
                )
                peak = jnp.max(scores, axis=-1, keepdims=True)
                mixed = mix(jnp.exp(scores - peak).astype(jnp.bfloat16), values)
                part[p, :, 0:128] = both(mixed[:, 0:128])
                part[p, :, 128:256] = both(mixed[:, 128:256])
                peaks[p] = jnp.broadcast_to(peak, (256, 128))

        @pl.when(t < 2)
        def _():
            own_part(2)

        @pl.when(t >= 2)
        def _():
            own_part(4)

        @pl.when((lane == 1) | (t > 0))
        def _():
            arrived(x_cross.at[t], cross_sem.at[t])

        normed[128:256] = rms(rows_of(x_cross.at[t]).astype(jnp.float32), gain)
        for c in range(CHUNKS):
            columns = slice(256 * c, 256 * (c + 1))
            k = jnp.dot(normed[128:256], wk[:, columns], preferred_element_type=jnp.float32)
            v = jnp.dot(normed[128:256], wv[:, columns], preferred_element_type=jnp.float32)
            for i in range(2):
                half = slice(128 * i, 128 * (i + 1))
                k_cross[2 * c + i] = k[:, half].astype(jnp.bfloat16)
                v_cross[2 * c + i] = v[:, half].astype(jnp.bfloat16)
        for p in range(PAIRS):
            scores = scores_of(p, k_cross[p]) + bias[t, 0:1, 0:128]
            earlier = peaks[p]
            peak = jnp.maximum(earlier, jnp.max(scores, axis=-1, keepdims=True))
            scale = jnp.exp(both(earlier - peak))
            added = mix(jnp.exp(scores - peak).astype(jnp.bfloat16), v_cross[p])
            over = part[p, :, 0:128] * scale + both(added[:, 0:128])
            under = part[p, :, 128:256] * scale + both(added[:, 128:256])
            ctx[p] = (over / under).astype(jnp.bfloat16)
        context = jnp.concatenate([ctx[p] for p in range(PAIRS)], axis=1)
        for c in range(CHUNKS):
            columns = slice(256 * c, 256 * (c + 1))
            mixed = jnp.dot(context, wo[:, columns], preferred_element_type=jnp.float32)
            x_out[t, c] = (x_own[t, c].astype(jnp.float32) + mixed).astype(jnp.bfloat16)

        @pl.when(seg < last)
        def _():
            for c in range(CHUNKS):
                remote(
                    x_out.at[t, c],
                    x_own.at[t, c],
                    send_own_sem.at[t],
                    own_sem.at[t, c],
                    seq,
                    seg + 1,
                ).start()

        @pl.when(seg == last)
        def _():
            final = rms(rows_of(x_out.at[t]).astype(jnp.float32), out_gain_ref[...])
            predicted = jnp.dot(final, w_read_ref[...], preferred_element_type=jnp.float32)
            block = 2 * t + lane
            pred_send[t] = predicted

            @pl.when((block != seq) | (member != last))
            def _():
                remote(
                    pred_send.at[t], pred_recv, pred_send_sem.at[t], pred_sem, block, member
                ).start()

            @pl.when((block == seq) & (member == last))
            def _():
                pred_recv[...] = predicted

            @pl.when(t != home)
            def _():
                pltpu.make_async_copy(obs.at[t], obs.at[t], obs_sem.at[t]).wait()

            errors = predicted - obs[t]
            hours = lax.broadcasted_iota(jnp.int32, (128, 128), 0) + block * 128
            weight = 1.0 + hours.astype(jnp.float32) * (2.0 / 2047.0)
            squares = weight * errors * errors
            acc[...] += jnp.sum(squares.reshape(16, 8, 128), axis=0)

        return 0

    @pl.when(follows)
    def _():
        pl.semaphore_wait(token, 1)
        start_copy().start()

    @pl.when(leads)
    def _():
        start_copy().wait_send()
        signal(token, 2 * after + lane, 2 * ((plane + 1) % 3 + 1) + core)

    lax.fori_loop(0, TICKS, tick, 0)

    def send_fit(j, _):
        @pl.when((j != seq) | (member != last))
        def _():
            remote(
                fit_send, fit_recv.at[lane], fit_send_sem.at[j], fit_sem.at[lane], j, member
            ).start()

        return 0

    def sent_fit(j, _):
        @pl.when((j != seq) | (member != last))
        def _():
            remote(
                fit_send, fit_recv.at[lane], fit_send_sem.at[j], fit_sem.at[lane], j, member
            ).wait_send()

        return 0

    @pl.when(seg == last)
    def _():
        fit_send[...] = acc[...]
        lax.fori_loop(0, 16, send_fit, 0)

        @pl.when(member == last)
        def _():
            fit_recv[lane] = acc[...]

    def sent_tick(t, _):
        @pl.when(seg < last)
        def _():
            pltpu.make_async_copy(x_out.at[t], x_out.at[t], send_own_sem.at[t]).wait()

        @pl.when(t + lane < TICKS)
        def _():
            pltpu.make_async_copy(x_own.at[t], x_own.at[t], send_cross_sem.at[t]).wait()

        @pl.when(2 * t + lane != seq)
        def _():
            pltpu.make_async_copy(bias.at[home], bias.at[home], bias_send_sem.at[t]).wait()

        @pl.when(seg == last)
        def _():
            @pl.when(2 * t + lane != seq)
            def _():
                pltpu.make_async_copy(obs.at[home], obs.at[home], obs_send_sem.at[t]).wait()

            @pl.when((2 * t + lane != seq) | (member != last))
            def _():
                pltpu.make_async_copy(pred_send.at[t], pred_send.at[t], pred_send_sem.at[t]).wait()

        return 0

    lax.fori_loop(0, TICKS, sent_tick, 0)

    @pl.when((seg + home > 0) & jnp.logical_not(leads))
    def _():
        start_copy().wait_send()

    @pl.when(seg == last)
    def _():
        lax.fori_loop(0, 16, sent_fit, 0)

    @pl.when((seg != last) | (member != last))
    def _():
        pltpu.make_async_copy(pred_recv, pred_recv, pred_sem).wait()

    for source in range(2):

        @pl.when((seg != last) | (seq != 14 + source))
        def _():
            pltpu.make_async_copy(fit_recv.at[source], fit_recv.at[source], fit_sem.at[source]).wait()

    pred_out[...] = pred_recv[...]
    total = jnp.sum(fit_recv[0] + fit_recv[1])
    fit_out[0] = -total / (2048.0 * 128.0)


def per_device(
    base_state,
    forcing,
    theta_base,
    perturb,
    order,
    w_force,
    attn_gain,
    w_query,
    w_key,
    w_value,
    w_out,
    block_mask,
    out_gain,
    w_read,
    observed,
):
    vmem = pl.BlockSpec(memory_space=pltpu.VMEM)
    smem = pl.BlockSpec(memory_space=pltpu.SMEM)
    hbm = pl.BlockSpec(memory_space=pl.ANY)
    bf16, f32 = jnp.bfloat16, jnp.float32
    dma = pltpu.SemaphoreType.DMA
    predictions, fitness = pl.pallas_call(
        kernel,
        out_shape=(
            jax.ShapeDtypeStruct((128, 128), f32),
            jax.ShapeDtypeStruct((1,), f32),
        ),
        in_specs=[hbm] * 15,
        out_specs=(vmem, smem),
        scratch_shapes=[
            pltpu.VMEM((128, 1024), bf16),
            pltpu.VMEM((64, 128), f32),
            pltpu.VMEM((1, 64), f32),
            pltpu.VMEM((32, 64), f32),
            pltpu.SMEM((32,), jnp.int32),
            pltpu.VMEM((64, 1024), bf16),
            pltpu.VMEM((1, 1024), f32),
            pltpu.SMEM((1, 4), jnp.int32),
            pltpu.VMEM((1, 1024), f32),
            pltpu.VMEM((1024, 128), bf16),
            pltpu.VMEM((1024, 1024), bf16),
            pltpu.VMEM((1024, 1024), bf16),
            pltpu.VMEM((1024, 1024), bf16),
            pltpu.VMEM((1024, 1024), bf16),
            pltpu.VMEM((TICKS, CHUNKS, 128, 256), bf16),
            pltpu.VMEM((TICKS, CHUNKS, 128, 256), bf16),
            pltpu.VMEM((TICKS, CHUNKS, 128, 256), bf16),
            pltpu.VMEM((CHUNKS, 128, 256), bf16),
            pltpu.VMEM((256, 1024), bf16),
            pltpu.VMEM((PAIRS, 256, 128), bf16),
            pltpu.VMEM((TICKS, PAIRS, 128, 128), bf16),
            pltpu.VMEM((TICKS, PAIRS, 128, 128), bf16),
            pltpu.VMEM((PAIRS, 128, 128), bf16),
            pltpu.VMEM((PAIRS, 128, 128), bf16),
            pltpu.VMEM((PAIRS, 128, 128), bf16),
            pltpu.VMEM((PAIRS, 128, 256), f32),
            pltpu.VMEM((PAIRS, 256, 128), f32),
            pltpu.VMEM((256, 128), f32),
            pltpu.VMEM((TICKS, 8, 512), f32),
            pltpu.VMEM((TICKS, 128, 128), f32),
            pltpu.VMEM((TICKS, 128, 128), f32),
            pltpu.VMEM((128, 128), f32),
            pltpu.VMEM((8, 128), f32),
            pltpu.VMEM((8, 128), f32),
            pltpu.VMEM((2, 8, 128), f32),
            dma((15,)),
            dma((TICKS, CHUNKS)),
            dma((TICKS,)),
            dma((TICKS,)),
            dma((TICKS,)),
            dma,
            dma((TICKS,)),
            dma((8,)),
            dma((TICKS,)),
            dma((8,)),
            dma,
            dma((TICKS,)),
            dma((2,)),
            dma((16,)),
            pltpu.SemaphoreType.REGULAR,
        ],
        compiler_params=pltpu.CompilerParams(
            has_side_effects=True, collective_id=0, vmem_limit_bytes=60 * 1024 * 1024
        ),
    )(
        base_state,
        forcing.T,
        theta_base.reshape(1, -1),
        perturb,
        order,
        w_force,
        attn_gain,
        w_query,
        w_key,
        w_value,
        w_out,
        block_mask,
        out_gain.reshape(1, -1),
        w_read,
        observed,
    )
    return predictions[None], fitness


def solution(mesh):
    placed = (
        P("seq", None),
        P("seq", None),
        P(),
        P(),
        P(),
        P(),
        P("segment", None),
        P("segment", None, None),
        P("segment", None, None),
        P("segment", None, None),
        P("segment", None, None),
        P("seq", None),
        P(),
        P(),
        P("seq", None),
    )
    return jax.shard_map(
        per_device,
        mesh=mesh,
        in_specs=placed,
        out_specs=(P("segment", "seq", None), P("segment")),
        check_vma=False,
    )
```

```python
import jax
import jax.numpy as jnp
from jax import lax
from jax.experimental import pallas as pl
from jax.experimental.pallas import tpu as pltpu
from jax.sharding import PartitionSpec as P

TICKS = 8
PAIRS = 8
CHUNKS = 4
NEG = -1e30


def rms(values, gain):
    meansq = jnp.mean(values * values, axis=-1, keepdims=True) + 1e-05
    return (values * lax.rsqrt(meansq) * gain).astype(jnp.bfloat16)


def rows_of(ref):
    return jnp.concatenate([ref[c] for c in range(CHUNKS)], axis=1)


def kernel(
    base_hbm,
    forcing_hbm,
    theta_hbm,
    perturb_hbm,
    order_hbm,
    w_force_hbm,
    gain_hbm,
    wq_hbm,
    wk_hbm,
    wv_hbm,
    wo_hbm,
    mask_hbm,
    out_gain_hbm,
    w_read_hbm,
    observed_hbm,
    pred_out,
    fit_out,
    base_ref,
    forcing_ref,
    theta_ref,
    perturb_ref,
    order_ref,
    w_force_ref,
    gain_ref,
    mask_ref,
    out_gain_ref,
    w_read_ref,
    wq,
    wk,
    wv,
    wo,
    x_own,
    x_cross,
    x_out,
    starts,
    normed,
    q_buf,
    k_own,
    v_own,
    k_cross,
    v_cross,
    ctx,
    part,
    peaks,
    causal,
    bias,
    obs,
    pred_send,
    pred_recv,
    acc,
    fit_send,
    fit_recv,
    w_sem,
    own_sem,
    cross_sem,
    send_own_sem,
    send_cross_sem,
    start_sem,
    bias_sem,
    bias_send_sem,
    obs_sem,
    obs_send_sem,
    pred_sem,
    pred_send_sem,
    fit_sem,
    fit_send_sem,
    token,
):
    seq = lax.axis_index("seq")
    seg = lax.axis_index("segment")
    lane = seq % 2
    member = seq // 2
    home = seq // 2
    other = seq + 1 - 2 * lane
    last = 7

    def remote(src, dst, send, recv, to_seq, to_seg):
        return pltpu.make_async_remote_copy(
            src_ref=src,
            dst_ref=dst,
            send_sem=send,
            recv_sem=recv,
            device_id={"seq": to_seq, "segment": to_seg},
            device_id_type=pl.DeviceIdType.MESH,
        )

    first = [
        (base_hbm, base_ref),
        (forcing_hbm, forcing_ref),
        (theta_hbm, theta_ref),
        (perturb_hbm, perturb_ref),
        (order_hbm, order_ref),
        (w_force_hbm, w_force_ref),
    ]
    second = [
        (mask_hbm, mask_ref),
        (gain_hbm, gain_ref),
        (wq_hbm.at[0], wq),
        (wk_hbm.at[0], wk),
        (wv_hbm.at[0], wv),
        (wo_hbm.at[0], wo),
        (out_gain_hbm, out_gain_ref),
        (w_read_hbm, w_read_ref),
        (observed_hbm, obs.at[home]),
    ]
    def signal(sem, to_seq, to_seg):
        pl.semaphore_signal(
            sem,
            inc=1,
            device_id={"seq": to_seq, "segment": to_seg},
            device_id_type=pl.DeviceIdType.MESH,
        )

    def arrived(ref, sem):
        pltpu.make_async_copy(ref, ref, sem).wait()

    loads = [
        pltpu.make_async_copy(source, target, w_sem.at[i])
        for i, (source, target) in enumerate(first + second)
    ]
    for load in loads[: len(first)]:
        load.start()

    plane = seg // 2
    core = seg % 2
    slot = 2 * ((plane + 8 - home) % 4) + core
    before = home - 3 + plane // 3
    after = home + 3 - (plane % 2) * (1 - plane // 3)
    follows = (plane > 0) & (before >= 0)
    leads = (plane > 0) & (after < 8)

    barrier = pltpu.get_barrier_semaphore()
    ends = seg // last

    @pl.when(seg > 0)
    def _():
        signal(barrier, seq, seg - 1)

    signal(barrier, other, seg)

    def greet(t, _):
        source = 2 * t + lane

        @pl.when(source != seq)
        def _():
            signal(barrier, source, seg)

        @pl.when((seg == 0) & ((home > 0) | (t > 0)))
        def _():
            signal(barrier, source, 2 * ((member // 2 + t) % 4) + member % 2)

        return 0

    lax.fori_loop(0, TICKS, greet, 0)

    @pl.when(follows)
    def _():
        signal(barrier, 2 * before + lane, 2 * (plane % 3 + 1) + core)

    for source in range(2):

        @pl.when((seq != 2 * seg + source) | (seg != last))
        def _():
            signal(barrier, 2 * seg + source, last)

    expected = 10 - ends
    expected += ((plane + 2) // 3) * (1 - after // 8)
    expected += ends * (16 - member // last)
    expected -= 1 - (seg + home + 13) // 14
    for load in loads[: len(first)]:
        load.wait()
    for load in loads[len(first) :]:
        load.start()

    def start_copy():
        return remote(starts, x_own.at[home], start_sem, own_sem.at[home, 0], 2 * slot + lane, 0)

    theta = theta_ref[...] + 0.5 * perturb_ref[pl.ds(order_ref[slot], 1), :]
    drive = forcing_ref[...].T * theta
    high = drive.astype(jnp.bfloat16)
    rest = drive - high.astype(jnp.float32)
    middle = rest.astype(jnp.bfloat16)
    low = (rest - middle.astype(jnp.float32)).astype(jnp.bfloat16)
    pl.semaphore_wait(barrier, expected)

    for c in range(CHUNKS):
        columns = slice(256 * c, 256 * (c + 1))
        w = w_force_ref[:, columns]
        lifted = jnp.dot(low, w, preferred_element_type=jnp.float32)
        lifted += jnp.dot(middle, w, preferred_element_type=jnp.float32)
        lifted += jnp.dot(high, w, preferred_element_type=jnp.float32)
        starts[c] = (base_ref[:, columns].astype(jnp.float32) + lifted).astype(jnp.bfloat16)

        @pl.when((seg + home > 0) & jnp.logical_not(follows))
        def _():
            remote(
                starts.at[c], x_own.at[home, c], start_sem, own_sem.at[home, 0], 2 * slot + lane, 0
            ).start()

    @pl.when((seg == 0) & (home == 0))
    def _():
        x_own[0] = starts[...]


    for load in loads[len(first) :]:
        load.wait()

    for level in range(4):
        usable = (mask_ref[0, level] == 1) & (seq >= 2**level)
        row = jnp.full((8, 128), jnp.where(usable, 0.0, NEG), jnp.float32)
        bias[home, :, 128 * level : 128 * (level + 1)] = row

    def send_bias(j, _):
        target = 2 * j + lane

        @pl.when(target != seq)
        def _():
            remote(
                bias.at[home], bias.at[home], bias_send_sem.at[j], bias_sem.at[home], target, seg
            ).start()

        return 0

    lax.fori_loop(0, 8, send_bias, 0)

    def send_obs(j, _):
        target = 2 * j + lane

        @pl.when(target != seq)
        def _():
            remote(
                obs.at[home], obs.at[home], obs_send_sem.at[j], obs_sem.at[home], target, last
            ).start()

        return 0

    @pl.when(seg == last)
    def _():
        lax.fori_loop(0, 8, send_obs, 0)

    row = lax.broadcasted_iota(jnp.int32, (256, 128), 0) % 128
    column = lax.broadcasted_iota(jnp.int32, (256, 128), 1)
    causal[...] = jnp.where(column <= row, 0.0, NEG)
    acc[...] = jnp.zeros_like(acc)

    @pl.when(lane == 0)
    def _():
        x_cross[0] = jnp.zeros_like(x_cross[0])

    left = lax.broadcasted_iota(jnp.int32, (128, 128), 1) < 64

    def tick(t, _):
        def hand_on(c):
            remote(
                x_own.at[t, c],
                x_cross.at[t + lane, c],
                send_cross_sem.at[t],
                cross_sem.at[t + lane],
                other,
                seg,
            ).start()

        @pl.when((seg == 0) & (t + home > 0))
        def _():
            arrived(x_own.at[t], own_sem.at[t, 0])

        @pl.when((seg == 0) & (t + lane < TICKS))
        def _():
            for c in range(CHUNKS):
                hand_on(c)

        @pl.when((seg > 0) & (t + lane < TICKS))
        def _():
            for c in range(CHUNKS):
                arrived(x_own.at[t, c], own_sem.at[t, c])
                hand_on(c)

        @pl.when((seg > 0) & (t + lane >= TICKS))
        def _():
            for c in range(CHUNKS):
                arrived(x_own.at[t, c], own_sem.at[t, c])

        @pl.when(t != home)
        def _():
            arrived(bias.at[t], bias_sem.at[t])

        gain = gain_ref[...]

        def scores_of(p, keys):
            return lax.dot_general(
                q_buf[p], keys, (((1,), (1,)), ((), ())), preferred_element_type=jnp.float32
            )

        def mix(expon, values):
            ones = jnp.ones((values.shape[0], 128), jnp.bfloat16)
            return jnp.dot(
                expon, jnp.concatenate([values, ones], axis=1), preferred_element_type=jnp.float32
            )

        def both(pair):
            return jnp.where(left, pair[0:128], pair[128:256])

        def own_part(levels):
            normed[0:128] = rms(rows_of(x_own.at[t]).astype(jnp.float32), gain)
            for c in range(CHUNKS):
                columns = slice(256 * c, 256 * (c + 1))
                mine = normed[0:128]
                q = jnp.dot(mine, wq[:, columns], preferred_element_type=jnp.float32) * 0.125
                k = jnp.dot(mine, wk[:, columns], preferred_element_type=jnp.float32)
                v = jnp.dot(mine, wv[:, columns], preferred_element_type=jnp.float32)
                for i in range(2):
                    p = 2 * c + i
                    half = slice(128 * i, 128 * (i + 1))
                    q_buf[p, 0:128] = jnp.where(left, q[:, half], 0.0).astype(jnp.bfloat16)
                    q_buf[p, 128:256] = jnp.where(left, 0.0, q[:, half]).astype(jnp.bfloat16)
                    k_own[t, p] = k[:, half].astype(jnp.bfloat16)
                    v_own[t, p] = v[:, half].astype(jnp.bfloat16)
            behind = [jnp.maximum(t - offset, 0) for offset in (1, 2, 4)[: levels - 1]]
            for p in range(PAIRS):
                keys = jnp.concatenate([k_own[t, p]] + [k_own[index, p] for index in behind], axis=0)
                values = jnp.concatenate(
                    [v_own[t, p]] + [v_own[index, p] for index in behind], axis=0
                )
                scores = scores_of(p, keys)
                scores = jnp.concatenate(
                    [
                        scores[:, 0:128] + causal[...],
                        scores[:, 128:] + bias[t, 0:1, 128 : 128 * levels],
                    ],
                    axis=1,
                )
                peak = jnp.max(scores, axis=-1, keepdims=True)
                mixed = mix(jnp.exp(scores - peak).astype(jnp.bfloat16), values)
                part[p, :, 0:128] = both(mixed[:, 0:128])
                part[p, :, 128:256] = both(mixed[:, 128:256])
                peaks[p] = jnp.broadcast_to(peak, (256, 128))

        @pl.when(t < 2)
        def _():
            own_part(2)

        @pl.when(t >= 2)
        def _():
            own_part(4)

        @pl.when((lane == 1) | (t > 0))
        def _():
            arrived(x_cross.at[t], cross_sem.at[t])

        normed[128:256] = rms(rows_of(x_cross.at[t]).astype(jnp.float32), gain)
        for c in range(CHUNKS):
            columns = slice(256 * c, 256 * (c + 1))
            k = jnp.dot(normed[128:256], wk[:, columns], preferred_element_type=jnp.float32)
            v = jnp.dot(normed[128:256], wv[:, columns], preferred_element_type=jnp.float32)
            for i in range(2):
                half = slice(128 * i, 128 * (i + 1))
                k_cross[2 * c + i] = k[:, half].astype(jnp.bfloat16)
                v_cross[2 * c + i] = v[:, half].astype(jnp.bfloat16)
        for p in range(PAIRS):
            scores = scores_of(p, k_cross[p]) + bias[t, 0:1, 0:128]
            earlier = peaks[p]
            peak = jnp.maximum(earlier, jnp.max(scores, axis=-1, keepdims=True))
            scale = jnp.exp(both(earlier - peak))
            added = mix(jnp.exp(scores - peak).astype(jnp.bfloat16), v_cross[p])
            over = part[p, :, 0:128] * scale + both(added[:, 0:128])
            under = part[p, :, 128:256] * scale + both(added[:, 128:256])
            ctx[p] = (over / under).astype(jnp.bfloat16)
        context = jnp.concatenate([ctx[p] for p in range(PAIRS)], axis=1)
        for c in range(CHUNKS):
            columns = slice(256 * c, 256 * (c + 1))
            mixed = jnp.dot(context, wo[:, columns], preferred_element_type=jnp.float32)
            x_out[t, c] = (x_own[t, c].astype(jnp.float32) + mixed).astype(jnp.bfloat16)

        @pl.when(seg < last)
        def _():
            for c in range(CHUNKS):
                remote(
                    x_out.at[t, c],
                    x_own.at[t, c],
                    send_own_sem.at[t],
                    own_sem.at[t, c],
                    seq,
                    seg + 1,
                ).start()

        @pl.when(seg == last)
        def _():
            final = rms(rows_of(x_out.at[t]).astype(jnp.float32), out_gain_ref[...])
            predicted = jnp.dot(final, w_read_ref[...], preferred_element_type=jnp.float32)
            block = 2 * t + lane
            pred_send[t] = predicted

            @pl.when((block != seq) | (member != last))
            def _():
                remote(
                    pred_send.at[t], pred_recv, pred_send_sem.at[t], pred_sem, block, member
                ).start()

            @pl.when((block == seq) & (member == last))
            def _():
                pred_recv[...] = predicted

            @pl.when(t != home)
            def _():
                pltpu.make_async_copy(obs.at[t], obs.at[t], obs_sem.at[t]).wait()

            errors = predicted - obs[t]
            hours = lax.broadcasted_iota(jnp.int32, (128, 128), 0) + block * 128
            weight = 1.0 + hours.astype(jnp.float32) * (2.0 / 2047.0)
            squares = weight * errors * errors
            acc[...] += jnp.sum(squares.reshape(16, 8, 128), axis=0)

        return 0

    @pl.when(follows)
    def _():
        pl.semaphore_wait(token, 1)
        start_copy().start()

    @pl.when(leads)
    def _():
        start_copy().wait_send()
        signal(token, 2 * after + lane, 2 * ((plane + 1) % 3 + 1) + core)

    lax.fori_loop(0, TICKS, tick, 0)

    def send_fit(j, _):
        @pl.when((j != seq) | (member != last))
        def _():
            remote(
                fit_send, fit_recv.at[lane], fit_send_sem.at[j], fit_sem.at[lane], j, member
            ).start()

        return 0

    def sent_fit(j, _):
        @pl.when((j != seq) | (member != last))
        def _():
            remote(
                fit_send, fit_recv.at[lane], fit_send_sem.at[j], fit_sem.at[lane], j, member
            ).wait_send()

        return 0

    @pl.when(seg == last)
    def _():
        fit_send[...] = acc[...]
        lax.fori_loop(0, 16, send_fit, 0)

        @pl.when(member == last)
        def _():
            fit_recv[lane] = acc[...]

    def sent_tick(t, _):
        @pl.when(seg < last)
        def _():
            pltpu.make_async_copy(x_out.at[t], x_out.at[t], send_own_sem.at[t]).wait()

        @pl.when(t + lane < TICKS)
        def _():
            pltpu.make_async_copy(x_own.at[t], x_own.at[t], send_cross_sem.at[t]).wait()

        @pl.when(2 * t + lane != seq)
        def _():
            pltpu.make_async_copy(bias.at[home], bias.at[home], bias_send_sem.at[t]).wait()

        @pl.when(seg == last)
        def _():
            @pl.when(2 * t + lane != seq)
            def _():
                pltpu.make_async_copy(obs.at[home], obs.at[home], obs_send_sem.at[t]).wait()

            @pl.when((2 * t + lane != seq) | (member != last))
            def _():
                pltpu.make_async_copy(pred_send.at[t], pred_send.at[t], pred_send_sem.at[t]).wait()

        return 0

    lax.fori_loop(0, TICKS, sent_tick, 0)

    @pl.when((seg + home > 0) & jnp.logical_not(leads))
    def _():
        start_copy().wait_send()

    @pl.when(seg == last)
    def _():
        lax.fori_loop(0, 16, sent_fit, 0)

    @pl.when((seg != last) | (member != last))
    def _():
        pltpu.make_async_copy(pred_recv, pred_recv, pred_sem).wait()

    for source in range(2):

        @pl.when((seg != last) | (seq != 14 + source))
        def _():
            pltpu.make_async_copy(fit_recv.at[source], fit_recv.at[source], fit_sem.at[source]).wait()

    pred_out[...] = pred_recv[...]
    total = jnp.sum(fit_recv[0] + fit_recv[1])
    fit_out[0] = -total / (2048.0 * 128.0)


def per_device(
    base_state,
    forcing,
    theta_base,
    perturb,
    order,
    w_force,
    attn_gain,
    w_query,
    w_key,
    w_value,
    w_out,
    block_mask,
    out_gain,
    w_read,
    observed,
):
    vmem = pl.BlockSpec(memory_space=pltpu.VMEM)
    smem = pl.BlockSpec(memory_space=pltpu.SMEM)
    hbm = pl.BlockSpec(memory_space=pl.ANY)
    bf16, f32 = jnp.bfloat16, jnp.float32
    dma = pltpu.SemaphoreType.DMA
    predictions, fitness = pl.pallas_call(
        kernel,
        out_shape=(
            jax.ShapeDtypeStruct((128, 128), f32),
            jax.ShapeDtypeStruct((1,), f32),
        ),
        in_specs=[hbm] * 15,
        out_specs=(vmem, smem),
        scratch_shapes=[
            pltpu.VMEM((128, 1024), bf16),
            pltpu.VMEM((64, 128), f32),
            pltpu.VMEM((1, 64), f32),
            pltpu.VMEM((32, 64), f32),
            pltpu.SMEM((32,), jnp.int32),
            pltpu.VMEM((64, 1024), bf16),
            pltpu.VMEM((1, 1024), f32),
            pltpu.SMEM((1, 4), jnp.int32),
            pltpu.VMEM((1, 1024), f32),
            pltpu.VMEM((1024, 128), bf16),
            pltpu.VMEM((1024, 1024), bf16),
            pltpu.VMEM((1024, 1024), bf16),
            pltpu.VMEM((1024, 1024), bf16),
            pltpu.VMEM((1024, 1024), bf16),
            pltpu.VMEM((TICKS, CHUNKS, 128, 256), bf16),
            pltpu.VMEM((TICKS, CHUNKS, 128, 256), bf16),
            pltpu.VMEM((TICKS, CHUNKS, 128, 256), bf16),
            pltpu.VMEM((CHUNKS, 128, 256), bf16),
            pltpu.VMEM((256, 1024), bf16),
            pltpu.VMEM((PAIRS, 256, 128), bf16),
            pltpu.VMEM((TICKS, PAIRS, 128, 128), bf16),
            pltpu.VMEM((TICKS, PAIRS, 128, 128), bf16),
            pltpu.VMEM((PAIRS, 128, 128), bf16),
            pltpu.VMEM((PAIRS, 128, 128), bf16),
            pltpu.VMEM((PAIRS, 128, 128), bf16),
            pltpu.VMEM((PAIRS, 128, 256), f32),
            pltpu.VMEM((PAIRS, 256, 128), f32),
            pltpu.VMEM((256, 128), f32),
            pltpu.VMEM((TICKS, 8, 512), f32),
            pltpu.VMEM((TICKS, 128, 128), f32),
            pltpu.VMEM((TICKS, 128, 128), f32),
            pltpu.VMEM((128, 128), f32),
            pltpu.VMEM((8, 128), f32),
            pltpu.VMEM((8, 128), f32),
            pltpu.VMEM((2, 8, 128), f32),
            dma((15,)),
            dma((TICKS, CHUNKS)),
            dma((TICKS,)),
            dma((TICKS,)),
            dma((TICKS,)),
            dma,
            dma((TICKS,)),
            dma((8,)),
            dma((TICKS,)),
            dma((8,)),
            dma,
            dma((TICKS,)),
            dma((2,)),
            dma((16,)),
            pltpu.SemaphoreType.REGULAR,
        ],
        compiler_params=pltpu.CompilerParams(
            has_side_effects=True, collective_id=0, vmem_limit_bytes=60 * 1024 * 1024
        ),
    )(
        base_state,
        forcing.T,
        theta_base.reshape(1, -1),
        perturb,
        order,
        w_force,
        attn_gain,
        w_query,
        w_key,
        w_value,
        w_out,
        block_mask,
        out_gain.reshape(1, -1),
        w_read,
        observed,
    )
    return predictions[None], fitness


def solution(mesh):
    placed = (
        P("seq", None),
        P("seq", None),
        P(),
        P(),
        P(),
        P(),
        P("segment", None),
        P("segment", None, None),
        P("segment", None, None),
        P("segment", None, None),
        P("segment", None, None),
        P("seq", None),
        P(),
        P(),
        P("seq", None),
    )
    return jax.shard_map(
        per_device,
        mesh=mesh,
        in_specs=placed,
        out_specs=(P("segment", "seq", None), P("segment")),
        check_vma=False,
    )
```
